256 devices in a mesh: reg: 8 (over y, core), prod: 32 (over x, z).
Axes of the slice: x: 4, y: 4, z: 8, core: 2. Of those that a mesh axis runs over, the one named last changes fastest.
Arguments:
- bottom_series_predictions: float32 [256, 1024, 128], P('reg', 'prod'), may hold values from -6 to 6
- group_item_predictions: float32 [32, 1024, 128], P('reg', 'prod'), may hold values from -18 to 18
- area_class_predictions: float32 [256, 32, 128], P('reg', 'prod'), may hold values from -18 to 18
- group_class_predictions: float32 [32, 32, 128], P('reg'), may hold values from -48 to 48
- bottom_series_precision: float32 [256, 1024], P('reg', 'prod'), may hold values from 0.5 to 5
- group_item_precision: float32 [32, 1024], P('reg', 'prod'), may hold values from 0.02 to 0.5
- area_class_precision: float32 [256, 32], P('reg', 'prod'), may hold values from 0.02 to 0.5
- group_class_precision: float32 [32, 32], P('reg'), may hold values from 0.002 to 0.05
- group_area_partition: int32 [32, 128], replicated, may hold values from -1 to 255, as said below
- class_item_partition: int32 [32, 128], replicated, may hold values from -1 to 1023, as said below
Outputs:
- solution_field: float32 [256, 1024, 128], P('reg', 'prod')
- residual: float32 [256, 1024, 128], P('reg', 'prod')
The draws below stay inside these ranges and needn't reach their ends.
Inputs may be any that keep to these rules, and one draw needn't show every extreme that they name: `group_area_partition`: every region stands in exactly one row; each row holds its parent's regions in its first slots and -1 in the rest; a parent has 1 to 128 regions, and some parent has exactly 128. `class_item_partition`: every product stands in exactly one row; each row holds its category's products in its first slots and -1 in the rest; a category has 1 to 128 products, and some category has exactly 128.
All inputs are finite; a program needn't handle non-finite values.
Results may differ from the reference program's by a relative error of at most 0.00011.
Values sent between devices are 32-bit elements; how exact they have to be, the bound alone decides.
No kernel may reach another device: no remote copies, remote signals or barrier semaphores. Data moves between devices by JAX's collectives and lax.ppermute only.
A program may use at most 64 MiB of HBM per device.

```python
import math
import jax
import jax.numpy as jnp
from jax import lax

HORIZON_PERIODS = 128
AREA_GROUPS = 32
GOODS_CLASSES = 32
CHILD_SLOTS = 128
ITERATIONS = 2
AREA_NUMBER = 256
ITEM_NUMBER = 1024
REGION_MOST = 128
PRODUCT_MOST = 128


def children_table(key, items, groups, slots, most):
    order = jax.random.permutation(jax.random.fold_in(key, 11), items).astype(jnp.int32)
    others = groups - 1
    remain = items - most
    base = remain // others
    extra = remain % others
    rest = base + (jnp.arange(others, dtype=jnp.int32) < extra).astype(jnp.int32)
    pairs = others // 2
    halves = jax.random.randint(jax.random.fold_in(key, 12), (pairs,), -(base // 2), base // 2 + 1, dtype=jnp.int32)
    delta = jnp.stack([halves, -halves], axis=1).reshape(2 * pairs)
    delta = jnp.concatenate([delta, jnp.zeros((others - 2 * pairs,), jnp.int32)])
    rest = rest + delta
    chosen = jax.random.randint(jax.random.fold_in(key, 13), (), 0, groups, dtype=jnp.int32)
    group_ids = jnp.arange(groups, dtype=jnp.int32)
    source = jnp.clip(group_ids - (group_ids > chosen).astype(jnp.int32), 0, others - 1)
    counts = jnp.where(group_ids == chosen, most, rest[source]).astype(jnp.int32)
    starts = jnp.cumsum(counts) - counts
    slot = jnp.arange(slots, dtype=jnp.int32)
    where_at = starts[:, None] + slot[None, :]
    valid = slot[None, :] < counts[:, None]
    picked = order[jnp.clip(where_at, 0, items - 1)]
    return jnp.where(valid, picked, -1).astype(jnp.int32)


def draw_group_area_partition(key, part):
    return children_table(jax.random.fold_in(key, 101), AREA_NUMBER, AREA_GROUPS, CHILD_SLOTS, REGION_MOST)


def draw_class_item_partition(key, part):
    return children_table(jax.random.fold_in(key, 202), ITEM_NUMBER, GOODS_CLASSES, CHILD_SLOTS, PRODUCT_MOST)


def block_levels(key, shape, split, smallest, top_value):
    def one(position, blocks):
        steps = jax.random.uniform(jax.random.fold_in(jax.random.fold_in(key, 6), position), (blocks,), jnp.float32, smallest / len(split), top_value / len(split))
        return jnp.repeat(jnp.exp(steps), shape[position] // blocks).reshape((-1,) + (1,) * (len(shape) - position - 1))

    factor_of = one(*split[0])
    for cut in split[1:]:
        factor_of = factor_of * one(*cut)
    return factor_of


def centred(stream_key, extent, scale, most, shards=(), kind=jnp.bfloat16):
    result = scale * jax.random.normal(stream_key, extent, jnp.float32)
    if shards:
        result = result * block_levels(stream_key, extent, shards, -0.22, 0.18)
    return jnp.clip(result, -most, most).astype(kind)


def setup_inputs(seed: int = 0) -> dict:
    arg_keys = jax.random.split(jax.random.key(seed), 11)
    bottom_series_predictions = centred(arg_keys[0], (AREA_NUMBER, ITEM_NUMBER, HORIZON_PERIODS), 1.0, 6.0, ((0, 8), (1, 32)), jnp.float32)
    group_item_predictions = centred(arg_keys[1], (AREA_GROUPS, ITEM_NUMBER, HORIZON_PERIODS), 3.0, 18.0, ((0, 8), (1, 32)), jnp.float32)
    area_class_predictions = centred(arg_keys[2], (AREA_NUMBER, GOODS_CLASSES, HORIZON_PERIODS), 3.0, 18.0, ((0, 8), (1, 32)), jnp.float32)
    group_class_predictions = centred(arg_keys[3], (AREA_GROUPS, GOODS_CLASSES, HORIZON_PERIODS), 8.0, 48.0, ((0, 8),), jnp.float32)
    bottom_series_precision = jnp.clip(jnp.exp(math.log(5.0) - 2.3025851 * jax.random.uniform(arg_keys[4], (AREA_NUMBER, ITEM_NUMBER), jnp.float32) ** block_levels(arg_keys[4], (AREA_NUMBER, ITEM_NUMBER), ((0, 8), (1, 32)), -0.2, 0.2)), 0.5, 5.0)
    group_item_precision = jnp.clip(jnp.exp(math.log(0.5) - 3.218876 * jax.random.uniform(arg_keys[5], (AREA_GROUPS, ITEM_NUMBER), jnp.float32) ** block_levels(arg_keys[5], (AREA_GROUPS, ITEM_NUMBER), ((0, 8), (1, 32)), -0.2, 0.2)), 0.02, 0.5)
    area_class_precision = jnp.clip(jnp.exp(math.log(0.5) - 3.218876 * jax.random.uniform(arg_keys[6], (AREA_NUMBER, GOODS_CLASSES), jnp.float32) ** block_levels(arg_keys[6], (AREA_NUMBER, GOODS_CLASSES), ((0, 8), (1, 32)), -0.2, 0.2)), 0.02, 0.5)
    group_class_precision = jnp.clip(jnp.exp(math.log(0.05) - 3.218876 * jax.random.uniform(arg_keys[7], (AREA_GROUPS, GOODS_CLASSES), jnp.float32) ** block_levels(arg_keys[7], (AREA_GROUPS, GOODS_CLASSES), ((0, 8),), -0.2, 0.2)), 0.002, 0.05)
    group_area_partition = draw_group_area_partition(jax.random.fold_in(arg_keys[10], 71), 0)
    class_item_partition = draw_class_item_partition(jax.random.fold_in(arg_keys[10], 71), 0)
    return {"bottom_series_predictions": bottom_series_predictions, "group_item_predictions": group_item_predictions, "area_class_predictions": area_class_predictions, "group_class_predictions": group_class_predictions, "bottom_series_precision": bottom_series_precision, "group_item_precision": group_item_precision, "area_class_precision": area_class_precision, "group_class_precision": group_class_precision, "group_area_partition": group_area_partition, "class_item_partition": class_item_partition}


def member_map(table, count):
    items = jnp.arange(count, dtype=jnp.int32)
    return jnp.any(table[:, :, None] == items[None, None, :], axis=1).astype(jnp.float32)


def aggregate_upward(area_index_table, item_index_table, upper, lower, corner):
    high = lax.Precision.HIGHEST
    widened = upper + jnp.einsum('pch,cq->pqh', corner, item_index_table, precision=high)
    first = jnp.einsum('pr,pqh->rqh', area_index_table, widened, precision=high)
    second = jnp.einsum('rch,cq->rqh', lower, item_index_table, precision=high)
    return first + second


def reference(bottom_series_predictions, group_item_predictions, area_class_predictions, group_class_predictions, bottom_series_precision, group_item_precision, area_class_precision, group_class_precision, group_area_partition, class_item_partition):
    high = lax.Precision.HIGHEST
    area_index_table = member_map(group_area_partition, AREA_NUMBER)
    item_index_table = member_map(class_item_partition, ITEM_NUMBER)

    def operate(field):
        row_total = jnp.einsum('pr,rqh->pqh', area_index_table, field, precision=high)
        col_total = jnp.einsum('cq,rqh->rch', item_index_table, field, precision=high)
        corner_total = jnp.einsum('pqh,cq->pch', row_total, item_index_table, precision=high)
        disaggregate_onto = aggregate_upward(area_index_table, item_index_table, group_item_precision[:, :, None] * row_total, area_class_precision[:, :, None] * col_total, group_class_precision[:, :, None] * corner_total)
        return bottom_series_precision[:, :, None] * field + disaggregate_onto

    system_source_term = bottom_series_precision[:, :, None] * bottom_series_predictions + aggregate_upward(area_index_table, item_index_table, group_item_precision[:, :, None] * group_item_predictions, area_class_precision[:, :, None] * area_class_predictions, group_class_precision[:, :, None] * group_class_predictions)
    solution_field = jnp.zeros_like(system_source_term)
    residual, direction = system_source_term, system_source_term
    norm_now = jnp.sum(residual * residual)
    for step in range(ITERATIONS):
        image = operate(direction)
        alpha = norm_now / jnp.sum(direction * image)
        solution_field = solution_field + alpha * direction
        residual = residual - alpha * image
        norm_next = jnp.sum(residual * residual)
        direction = residual + (norm_next / norm_now) * direction
        norm_now = norm_next
    return solution_field, residual
```

```python
import jax
import jax.numpy as jnp
from jax import lax
from jax.experimental import pallas as pl
from jax.experimental.pallas import tpu as pltpu
from jax.sharding import Mesh
from jax.sharding import PartitionSpec as P

F32 = jnp.float32
BF16 = jnp.bfloat16
REG = ("y", "core")
PROD = ("x", "z")
SPLIT = ("y", "core", "x")
GROUPS = 32
HIGH = lax.Precision.HIGHEST


def iota(shape, dim):
    return lax.broadcasted_iota(jnp.int32, shape, dim)


def parts(value):
    high = value.astype(BF16)
    rest = value - high.astype(F32)
    middle = rest.astype(BF16)
    return high, middle, (rest - middle.astype(F32)).astype(BF16)


def left_dot(flags, value):
    return sum(jnp.dot(flags, p, preferred_element_type=F32) for p in parts(value))


def right_dot(value, flags):
    return sum(jnp.dot(p, flags, preferred_element_type=F32) for p in parts(value))


def over_lanes(flags, value):
    dims = (((1,), (1,)), ((), ()))
    return sum(lax.dot_general(flags, p, dims, preferred_element_type=F32) for p in parts(value))


def over_rows(value, flags):
    dims = (((0,), (0,)), ((), ()))
    return sum(lax.dot_general(p, flags, dims, preferred_element_type=F32) for p in parts(value))


def swapped(pieces):
    group = iota(pieces[0].shape, 1) // 32
    odd, upper = (group & 1) == 1, group >= 2
    a = []
    for i in (0, 2):
        a.append(jnp.where(odd, pltpu.roll(pieces[i + 1], 32, 1), pieces[i]))
        a.append(jnp.where(odd, pieces[i + 1], pltpu.roll(pieces[i], 96, 1)))
    return (
        jnp.where(upper, pltpu.roll(a[2], 64, 1), a[0]),
        jnp.where(upper, pltpu.roll(a[3], 64, 1), a[1]),
        jnp.where(upper, a[2], pltpu.roll(a[0], 64, 1)),
        jnp.where(upper, a[3], pltpu.roll(a[1], 64, 1)),
    )


def class_flags(places):
    row = iota((64, 128), 0)
    at = (row // 8) * 4 + row % 4 == places
    second = (row & 4) == 4
    one, none = jnp.ones((64, 128), F32), jnp.zeros((64, 128), F32)
    first_flags = jnp.where(at, jnp.where(second, none, one), none)
    second_flags = jnp.where(at, jnp.where(second, one, none), none)
    return first_flags.astype(BF16), second_flags.astype(BF16)


def weighted(field, precision):
    return (field.reshape(32, 4, 8, 128) * precision.reshape(32, 1, 8, 128)).reshape(1024, 128)


def region_mix(field, precision, group_precision, flags, flags_t):
    return weighted(field, precision) + left_dot(
        flags_t, group_precision * left_dot(flags, field)
    )


def pack_kernel(b, d, gi, w1, ac, w2, gc, w3, out, turned):
    own = lax.axis_index("x") * 8 + lax.axis_index("z")
    for i in range(8):
        turned[pl.ds(i, 128, stride=8), :] = b[i * 128 : (i + 1) * 128, :].T
    d_flat = jnp.concatenate([d[pl.ds(k, 8, stride=4), :] for k in range(4)], axis=1)
    w1_flat = jnp.concatenate([w1[k : k + 1, :] for k in range(4)], axis=1)
    gi_turned = gi[...].T
    mine = (iota((4, 32, 128), 1) == own).astype(F32)
    corner = jnp.sum(gc[...] * mine, axis=1)
    corner_weight = jnp.sum(
        jnp.where(iota((4, 32), 1) == own, w3[...], 0.0), axis=1, keepdims=True
    )
    row, lane = iota((32, 128), 0), iota((32, 128), 1)
    place = ((row % 4 == lane // 32) & (row // 4 == lane % 8)).astype(F32)
    w2_row = jnp.sum(w2[...] * place, axis=0, keepdims=True)
    row, lane = iota((4, 128), 0), iota((4, 128), 1)
    place_corner = ((lane < 16) & (lane // 4 == row)).astype(F32)
    w3_row = jnp.sum(
        corner_weight * ((lane >= 16) & (lane < 32) & (lane // 4 - 4 == row)).astype(F32),
        axis=0,
        keepdims=True,
    )
    dims = (((0,), (0,)), ((), ()))
    row, lane = iota((128, 128), 0), iota((128, 128), 1)
    a = lax.dot_general(ac[...], place, dims, precision=HIGH, preferred_element_type=F32)
    a = jnp.where(row % 4 == (lane // 8) % 4, a, 0.0)
    z = lax.dot_general(
        corner * corner_weight, place_corner, dims, precision=HIGH, preferred_element_type=F32
    )
    z = jnp.where(row % 4 == lane % 4, z, 0.0)
    fold = (iota((32, 128), 1) // 4 == iota((32, 128), 0)).astype(F32)
    a = jnp.dot(fold, a, precision=HIGH, preferred_element_type=F32) * w2_row
    z = jnp.dot(fold, z, precision=HIGH, preferred_element_type=F32) + w3_row
    for s in range(32):
        out[s, 0:32, :] = turned[s * 32 : (s + 1) * 32, :]
        out[s, 32:40, :] = d_flat
        out[s, 40:44, :] = gi_turned[s * 4 : (s + 1) * 4, :]
        out[s, 44:45, :] = w1_flat
        out[s, 45:46, :] = a[s : s + 1, :]
        out[s, 46:47, :] = w2_row
        out[s, 47:48, :] = z[s : s + 1, :]


def spread_kernel(
    got, kap, gam, out, field_out, d_out, w1_out, flags_out, flags_t_out, own_out, s_ref, y_ref
):
    lane4 = iota((4, 128), 1)
    corner, corner_weight = jnp.zeros((4, 128), F32), jnp.zeros((4, 128), F32)
    own_out[...] = jnp.zeros_like(own_out)
    for g in range(8):
        pieces = swapped([got[g * 4 + x] for x in range(4)])
        for k in range(4):
            piece = pieces[k]
            d_out[(g * 4 + k) * 8 : (g * 4 + k + 1) * 8, :] = piece[32:40]
            for h in range(4):
                at = g * 128 + k * 32 + h * 8
                s_ref[at : at + 8, :] = piece[h * 8 : (h + 1) * 8] * piece[32:40]
            at = g * 16 + k * 4
            y_ref[at : at + 4, :] = piece[40:44] * piece[44:45]
            w1_out[at : at + 4, :] = jnp.broadcast_to(piece[44:45], (4, 128))
        lanes = slice(g * 128, (g + 1) * 128)
        z = jnp.concatenate([got[g * 4 + x, 47:48, :] for x in range(4)], axis=0)
        corner += pltpu.roll(jnp.where(lane4 < 16, z, 0.0), g * 16, 1)
        corner_weight += pltpu.roll(
            jnp.where((lane4 >= 16) & (lane4 < 32), z, 0.0), (g * 16 + 112) % 128, 1
        )
        for x in range(4):
            own_out[x : x + 1, lanes] = got[g * 4 + x, 45:46, :]
            own_out[8 + x : 9 + x, lanes] = got[g * 4 + x, 46:47, :]
    flags32 = (iota((128, 1024), 0) == kap[...]).astype(F32)
    flags, flags_t = flags32.astype(BF16), flags32.T.astype(BF16)
    flags_out[...] = flags
    flags_t_out[...] = flags_t
    own_out[0:4, :] += right_dot(corner, flags)
    own_out[16:20, 0:128] = corner_weight
    c0, c1 = class_flags(gam[...])
    w1, d = w1_out[...], d_out[...]
    field = s_ref[...] + left_dot(flags_t, y_ref[...])
    field_out[...] = field
    y0 = own_out[0:8, :]
    total = over_lanes(c0, field)
    field = region_mix(field, d, w1, flags, flags_t)
    total += over_lanes(c1, field)
    field = region_mix(field, d, w1, flags, flags_t)
    last = over_lanes(c0, field)
    y0 = pltpu.roll(y0, 4, 0)
    members = jnp.sum(flags32, axis=1, keepdims=True)
    w1_lifted = left_dot(flags_t, w1).reshape(32, 4, 8, 128)[:, 0].reshape(256, 128)
    small = []
    for v in (d, d * d, d * w1_lifted):
        small.append(over_lanes(c0, v[0:128]) + over_lanes(c1, v[128:256]))
    small.append(over_lanes(c0, w1) + over_lanes(c1, members * w1 * w1))
    for z in range(8):
        rows = slice(z * 8, (z + 1) * 8)
        for t in range(8):
            lanes = slice(t * 128, (t + 1) * 128)
            out[z, t * 8 : (t + 1) * 8, :] = total[rows, lanes]
            out[z, 64 + t * 8 : 64 + (t + 1) * 8, :] = last[rows, lanes] + y0[:, lanes]
        for j in range(4):
            out[z, 128 + j * 8 : 128 + (j + 1) * 8, :] = small[j][rows]


def stacked(ref, first):
    rows = [
        jnp.concatenate(
            [ref[z, first + t * 8 : first + (t + 1) * 8, :] for t in range(8)], axis=1
        )
        for z in range(8)
    ]
    return jnp.concatenate(rows, axis=0)


def row_sums(value):
    rows = jnp.sum(value, axis=0, keepdims=True)
    return sum(rows[:, t * 128 : (t + 1) * 128] for t in range(value.shape[1] // 128))


def middle_kernel(
    got, field_in, d_in, w1_in, flags_in, flags_t_in, own, sizes, gam, out, r0_out, br_out
):
    flags, flags_t, d, w1 = flags_in[...], flags_t_in[...], d_in[...], w1_in[...]
    top = iota((8, 1024), 0) < 4
    top_small = iota((8, 128), 0) < 4

    def upper(value):
        return jnp.where(top if value.shape[1] == 1024 else top_small, value, 0.0)

    def lower(value):
        return upper(pltpu.roll(value, 4, 0))

    def row(first):
        return jnp.concatenate(
            [
                sum(got[z, first + t * 8 : first + (t + 1) * 8, :] for z in range(8))
                for t in range(8)
            ],
            axis=1,
        )

    small = [sum(got[z, 128 + j * 8 : 136 + j * 8, :] for z in range(8)) for j in range(4)]
    tile_row, tile_lane = iota((128, 1024), 0), iota((128, 1024), 1)
    from_at = (tile_lane // 32) * 8 + tile_lane % 8
    first = (from_at == tile_row).astype(F32).astype(BF16)
    second = (from_at == tile_row + 128).astype(F32).astype(BF16)
    wide = right_dot(jnp.concatenate([upper(v) for v in small[:3]], axis=0), first)
    wide += right_dot(jnp.concatenate([lower(v) for v in small[:3]], axis=0), second)
    vd, vd2, e = wide[0:8], wide[8:16], wide[16:24]
    vw, vw2 = upper(small[3]), lower(small[3])
    v01, v2 = row(0), upper(row(64))
    v0, v1 = upper(v01), lower(v01)
    y0, w2, w3 = own[0:8, :], own[8:16, :], own[16:24, 0:128]
    n = jnp.concatenate([sizes[...]] * 8, axis=1)

    def up(value):
        return right_dot(value, flags_t)

    def down(value):
        return right_dot(value, flags)

    def shared(value):
        return w2 * value + down(w3 * up(value))

    sums = up(jnp.concatenate([y0, e * y0], axis=0))
    u0, ue = sums[0:8], sums[8:16]
    lifts = down(jnp.concatenate([u0, vw * u0, ue + vw2 * u0], axis=0))
    b1 = v1 + vd * y0 + lifts[8:16]
    b2 = v2 + vd2 * y0 + e * lifts[0:8] + lifts[16:24]
    g0 = v0 + n * y0
    y1 = shared(g0)
    g1 = b1 + n * y1
    y2 = shared(g1)
    k1 = vd * y1 + down(vw * up(y1))
    m1 = row_sums(g0 * y1)
    m2 = row_sums((2.0 * b1 + n * y1) * y1)
    m3 = row_sums((2.0 * b2 + k1) * y1 + g1 * y2)

    _, c1 = class_flags(gam[...])
    r0 = field_in[...] + over_rows(stacked(got, 64), c1)
    r0_out[...] = r0
    br = region_mix(r0, d, w1, flags, flags_t)
    br_out[...] = br
    bbr = region_mix(br, d, w1, flags, flags_t)
    m0 = row_sums(r0 * r0)
    m1 += row_sums(r0 * br)
    m2 += row_sums(br * br)
    m3 += row_sums(br * bbr)
    moments = jnp.concatenate([m0, m1, m2, m3, jnp.zeros((4, 128), F32)], axis=0)
    both = y1 + pltpu.roll(y2, 4, 0)
    for z in range(8):
        for t in range(8):
            out[z, t * 8 : (t + 1) * 8, :] = both[:, t * 128 : (t + 1) * 128]
        out[z, 64:72, :] = moments


def fields_kernel(got, r0_in, br_in, d_in, w1_in, flags_in, flags_t_in, gam, out, f_ref, g_ref):
    c0, c1 = class_flags(gam[...])
    shares = stacked(got, 0)
    field = br_in[...] + over_rows(shares, c0)
    f_ref[...] = field
    g_ref[...] = region_mix(
        field, d_in[...], w1_in[...], flags_in[...], flags_t_in[...]
    ) + over_rows(shares, c1)
    moments = sum(got[z, 64:72, :] for z in range(8))
    for g in range(8):
        for i, ref in enumerate((r0_in, f_ref, g_ref)):
            pieces = swapped([ref[g * 128 + k * 32 : g * 128 + (k + 1) * 32, :] for k in range(4)])
            for x in range(4):
                out[g * 4 + x, i * 32 : (i + 1) * 32, :] = pieces[x]
        for x in range(4):
            out[g * 4 + x, 96:104, :] = moments


def finish_kernel(got, x_out, r_out, x_ref, r_ref):
    tile = got[0, 96:104, :]
    for s in range(1, 32):
        tile += got[s, 96:104, :]
    m = jnp.sum(tile, axis=1, keepdims=True)
    m0, m1, m2, m3 = (m[i : i + 1, :] for i in range(4))
    alpha = m0 / m1
    norm = m0 - 2.0 * alpha * m1 + alpha * alpha * m2
    grown = 1.0 + norm / m0
    product = grown * grown * m1 - 2.0 * grown * alpha * m2 + alpha * alpha * m3
    later = norm / product
    on_first, on_second = alpha + later * grown, -later * alpha
    for s in range(32):
        first, second, third = got[s, 0:32, :], got[s, 32:64, :], got[s, 64:96, :]
        x_ref[s * 32 : (s + 1) * 32, :] = on_first * first + on_second * second
        r_ref[s * 32 : (s + 1) * 32, :] = first - on_first * second - on_second * third
    for i in range(8):
        x_out[i * 128 : (i + 1) * 128, :] = x_ref[pl.ds(i, 128, stride=8), :].T
        r_out[i * 128 : (i + 1) * 128, :] = r_ref[pl.ds(i, 128, stride=8), :].T


def call(kernel, outs, scratch=()):
    vmem = pl.BlockSpec(memory_space=pltpu.VMEM)
    return lambda *args: pl.pallas_call(
        kernel,
        out_shape=tuple(jax.ShapeDtypeStruct(shape, kind) for shape, kind in outs),
        in_specs=[vmem] * len(args),
        out_specs=(vmem,) * len(outs),
        scratch_shapes=[pltpu.VMEM(shape, F32) for shape in scratch],
    )(*args)


def exchanged(value, axes):
    return lax.all_to_all(value, axes, 0, 0, tiled=True)


def row_of(table, wanted, names):
    hit = table[:, :, None] == wanted[None, None, :]
    return jnp.sum(jnp.where(hit, names[:, None, None], 0), axis=(0, 1), dtype=jnp.int32)


def on_device(b, gi, ac, gc, d, w1, w2, w3, group_table, class_table):
    z = lax.axis_index("z")
    (sent,) = call(pack_kernel, [((32, 48, 128), F32)], [(1024, 128)])(
        b.reshape(1024, 128), d, gi.reshape(128, 128), w1, ac.reshape(32, 128), w2, gc, w3
    )
    got = exchanged(sent, SPLIT)

    parent = row_of(group_table, jnp.arange(256, dtype=jnp.int32), jnp.arange(32, dtype=jnp.int32))
    kap = parent.reshape(8, 8, 4).transpose(0, 2, 1)[:, :, None, :] * 4
    kap = (kap + jnp.arange(4, dtype=jnp.int32)[None, None, :, None]).reshape(1, 1024)
    lane = jnp.arange(128, dtype=jnp.int32)
    category = jnp.arange(32, dtype=jnp.int32)
    gam = row_of(
        class_table,
        (lane // 32) * 256 + z * 32 + lane % 32,
        (category % 8) * 4 + category // 8,
    ).reshape(1, 128)
    count = jnp.sum((class_table >= 0).astype(F32), axis=1).reshape(4, 8)
    count = jnp.sum(jnp.where(jnp.arange(8)[None, :] == z, count, 0.0), axis=1)
    sizes = jnp.broadcast_to(jnp.pad(count, (0, 4))[:, None], (8, 128))

    sent, field, d_all, w1_all, flags, flags_t, own = call(
        spread_kernel,
        [
            ((8, 160, 128), F32),
            ((1024, 128), F32),
            ((256, 128), F32),
            ((128, 128), F32),
            ((128, 1024), BF16),
            ((1024, 128), BF16),
            ((24, 1024), F32),
        ],
        [(1024, 128), (128, 128)],
    )(got, kap, gam)
    got = exchanged(sent, "z")
    sent, r0, br = call(
        middle_kernel, [((8, 72, 128), F32), ((1024, 128), F32), ((1024, 128), F32)]
    )(got, field, d_all, w1_all, flags, flags_t, own, sizes, gam)
    got = exchanged(sent, "z")
    (sent,) = call(fields_kernel, [((32, 104, 128), F32)], [(1024, 128), (1024, 128)])(
        got, r0, br, d_all, w1_all, flags, flags_t, gam
    )
    got = exchanged(sent, SPLIT)
    solution_field, residual = call(
        finish_kernel, [((1024, 128), F32)] * 2, [(1024, 128), (1024, 128)]
    )(got)
    return solution_field.reshape(32, 32, 128), residual.reshape(32, 32, 128)


def solution(mesh):
    finer = Mesh(mesh.devices.reshape(4, 2, 4, 8), ("y", "core", "x", "z"))
    return jax.shard_map(
        on_device,
        mesh=finer,
        in_specs=(
            P(REG, PROD, None),
            P(REG, PROD, None),
            P(REG, PROD, None),
            P(REG, None, None),
            P(REG, PROD),
            P(REG, PROD),
            P(REG, PROD),
            P(REG, None),
            P(),
            P(),
        ),
        out_specs=(P(REG, PROD, None), P(REG, PROD, None)),
        check_vma=False,
    )
```

```python
import jax
import jax.numpy as jnp
from jax import lax
from jax.experimental import pallas as pl
from jax.experimental.pallas import tpu as pltpu
from jax.sharding import Mesh
from jax.sharding import PartitionSpec as P

F32 = jnp.float32
BF16 = jnp.bfloat16
REG = ("y", "core")
PROD = ("x", "z")
SPLIT = ("y", "core", "x")
LANES = (((1,), (1,)), ((), ()))


def iota(shape, dim):
    return lax.broadcasted_iota(jnp.int32, shape, dim)


def flag(condition):
    return condition.astype(F32).astype(BF16)


def parts(value):
    high = value.astype(BF16)
    return high, (value - high.astype(F32)).astype(BF16)


def dot(a, b):
    if a.dtype == BF16:
        return sum(jnp.dot(a, p, preferred_element_type=F32) for p in parts(b))
    return sum(jnp.dot(p, b, preferred_element_type=F32) for p in parts(a))


def dot_t(value, flags):
    return sum(lax.dot_general(p, flags, LANES, preferred_element_type=F32) for p in parts(value))


def swapped(pieces):
    group = iota(pieces[0].shape, 1) // 32
    odd, upper = (group & 1) == 1, group >= 2
    a = []
    for i in (0, 2):
        a.append(jnp.where(odd, pltpu.roll(pieces[i + 1], 32, 1), pieces[i]))
        a.append(jnp.where(odd, pieces[i + 1], pltpu.roll(pieces[i], 96, 1)))
    return (
        jnp.where(upper, pltpu.roll(a[2], 64, 1), a[0]),
        jnp.where(upper, pltpu.roll(a[3], 64, 1), a[1]),
        jnp.where(upper, a[2], pltpu.roll(a[0], 64, 1)),
        jnp.where(upper, a[3], pltpu.roll(a[1], 64, 1)),
    )


def group_flags(parent):
    row = iota((128, 256), 0)
    return [flag(row == parent + 32 * h) for h in range(4)]


def category_flags(places):
    row = iota((128, 128), 0)
    return [flag(row == places * 4 + h) for h in range(4)]


def grouped(field, flags):
    return sum(dot_t(field[h], flags[h]) for h in range(4))


def ungrouped(value, flags):
    high, low = parts(value)
    return [
        jnp.dot(high, f, preferred_element_type=F32) + jnp.dot(low, f, preferred_element_type=F32)
        for f in flags
    ]


def mixed(field, precision, group_precision, flags):
    lifted = ungrouped(group_precision * grouped(field, flags), flags)
    return [precision * field[h] + lifted[h] for h in range(4)]


def categories(field, flags):
    return sum(dot(flags[h], field[h]) for h in range(4))


def lifted_categories(value, flags):
    high, low = parts(value)
    dims = (((0,), (0,)), ((), ()))
    return [
        lax.dot_general(f, high, dims, preferred_element_type=F32)
        + lax.dot_general(f, low, dims, preferred_element_type=F32)
        for f in flags
    ]


def steps(ref):
    return [ref[h * 128 : (h + 1) * 128, :] for h in range(4)]


def pack_kernel(b, d, gi, w1, ac, w2, gc, w3, out, turned, turned_small):
    own = lax.axis_index("x") * 8 + lax.axis_index("z")
    for i in range(8):
        block = jnp.concatenate(
            [b[pl.ds(k * 8 + i, 32, stride=32), :] for k in range(4)], axis=0
        )
        turned[pl.ds(i, 128, stride=8), :] = block.T
    d_turned = d[...].T
    d_rows = jnp.concatenate([d_turned[k * 8 : (k + 1) * 8] for k in range(4)], axis=1)
    w1_row = jnp.concatenate([w1[k : k + 1, :] for k in range(4)], axis=1)
    w2_row = jnp.concatenate([w2[...]] * 4, axis=1)
    gi_turned = gi[...].T
    mine = (iota((4, 32, 128), 1) == own).astype(F32)
    corner = jnp.sum(gc[...] * mine, axis=1)
    weight = jnp.sum(jnp.where(iota((4, 32), 1) == own, w3[...], 0.0), axis=1, keepdims=True)
    small = [ac[...], corner * weight, jnp.broadcast_to(weight, (4, 128))]
    small = jnp.concatenate([*small, jnp.zeros((88, 128), F32)], axis=0)
    turned_small[...] = small.T
    values = [turned_small[pl.ds(h, 32, stride=4), :] for h in range(4)]
    a = jnp.concatenate([v[:, 0:32] for v in values], axis=1) * w2_row
    z = jnp.concatenate([v[:, 32:64] for v in values], axis=1)
    for s in range(32):
        out[s, 0:32, :] = turned[s * 32 : (s + 1) * 32, :]
        out[s, 32:40, :] = d_rows
        out[s, 40:44, :] = gi_turned[s * 4 : (s + 1) * 4, :]
        out[s, 44:45, :] = w1_row
        out[s, 45:46, :] = a[s : s + 1, :]
        out[s, 46:47, :] = w2_row
        out[s, 47:48, :] = z[s : s + 1, :]


def spread_kernel(got, parent, gam, table, out, field_out, d_out, w1_out, own_out, g_ref, k_ref):
    for x in range(4):
        for half in range(2):
            lanes = slice(half * 128, (half + 1) * 128)
            pieces = swapped([got[(half * 4 + g) * 4 + x] for g in range(4)])
            for k in range(4):
                piece = pieces[k]
                at = x * 32 + k * 8
                d_out[at : at + 8, lanes] = piece[32:40]
                for h in range(4):
                    field_out[h * 128 + at : h * 128 + at + 8, lanes] = (
                        piece[h * 8 : (h + 1) * 8] * piece[32:40]
                    )
                for i in range(3):
                    own_out[i * 16 + x * 4 + k : i * 16 + x * 4 + k + 1, lanes] = piece[
                        45 + i : 46 + i
                    ]
    for g in range(8):
        pieces = swapped([got[g * 4 + x, 40:48, :] for x in range(4)])
        for k in range(4):
            g_ref[pl.ds(g * 4 + k, 4, stride=32), :] = pieces[k][0:4] * pieces[k][4:5]
            k_ref[pl.ds(g * 4 + k, 4, stride=32), :] = jnp.broadcast_to(
                pieces[k][4:5], (4, 128)
            )
    w1 = k_ref[...].T
    w1_out[...] = w1
    groups = group_flags(parent[...])
    flags = category_flags(gam[...])
    lane = iota((256, 256), 0)
    at = parent[...] // 4 * 32 + parent[...] % 4
    y0 = own_out[0:16, :] + dot(own_out[32:48, :], flag(lane == at))
    own_out[0:16, :] = y0
    d = d_out[...]
    lifted = ungrouped(g_ref[...].T, groups)
    field = [field_out[h * 128 : (h + 1) * 128, :] + lifted[h] for h in range(4)]
    for h in range(4):
        field_out[h * 128 : (h + 1) * 128, :] = field[h]
    totals = [categories(field, flags)]
    for _ in range(2):
        field = mixed(field, d, w1, groups)
        totals.append(categories(field, flags))
    plain = flag(iota((32, 128), 0) == gam[...])
    everywhere = flag(iota((128, 256), 0) % 32 == parent[...])
    members = lax.dot_general(
        jnp.ones((8, 256), BF16), everywhere, LANES, preferred_element_type=F32
    )[0:1]
    lifted_w1 = dot(w1, groups[0])
    small = [dot(plain, v) for v in (d, d * d, d * lifted_w1)]
    row, lane = iota((128, 256), 0), iota((128, 256), 1)
    at = jnp.where(row < 32, row // 4 * 32 + row % 4, -16)
    small.append(
        dot(dot(plain, w1), flag(lane == at + 4))
        + dot(dot(plain, members * w1 * w1), flag(lane == at + 8))
    )
    count = jnp.sum((table[...] >= 0).astype(F32), axis=1, keepdims=True)
    count = jnp.where(iota((32, 1), 0) % 8 == lax.axis_index("z"), count, 0.0)
    for x in range(4):
        size = jnp.sum(count[x * 8 : (x + 1) * 8], axis=0, keepdims=True)
        own_out[48 + x * 4 : 52 + x * 4, :] = jnp.broadcast_to(size, (4, 256))
    for z in range(8):
        for i in range(3):
            out[z, i * 16 : (i + 1) * 16, :] = totals[i][z * 16 : (z + 1) * 16]
        out[z, 48:64, :] = y0
        for i in range(4):
            out[z, 64 + i * 4 : 68 + i * 4, :] = small[i][z * 4 : (z + 1) * 4]


def lane_sums(value):
    rows = jnp.sum(value, axis=0, keepdims=True)
    return sum(rows[:, t * 128 : (t + 1) * 128] for t in range(value.shape[1] // 128))


def field_product(a, b):
    return lane_sums(sum(a[h] * b[h] for h in range(4)))


def middle_kernel(got, field_in, d_in, w1_in, own, parent, gam, out, r0_out, br_out):
    total = sum(got[z, 0:48, :] for z in range(8))
    small = sum(got[z, 64:80, :] for z in range(8))
    v0, v1, v2 = (total[i * 16 : (i + 1) * 16] for i in range(3))

    def repeated(first):
        rows = [
            jnp.broadcast_to(small[first + x : first + x + 1], (4, 256)) for x in range(4)
        ]
        return jnp.concatenate(rows, axis=0)

    vd, vd2, e, vw = (repeated(i * 4) for i in range(4))
    vw2 = pltpu.roll(vw, 252, 1)
    y0, w2, w3, n = (own[i * 16 : (i + 1) * 16, :] for i in range(4))
    at = parent[...] // 4 * 32 + parent[...] % 4 + 4
    places = flag(iota((256, 256), 0) == at)

    def up(value):
        return dot_t(value, places)

    def down(value):
        return dot(value, places)

    def shared(value):
        return w2 * value + down(w3 * up(value))

    sums = up(jnp.concatenate([y0, e * y0], axis=0))
    u0, ue = sums[0:16], sums[16:32]
    lifts = down(jnp.concatenate([u0, vw * u0, ue + vw2 * u0], axis=0))
    b1 = v1 + vd * y0 + lifts[16:32]
    b2 = v2 + vd2 * y0 + e * lifts[0:16] + lifts[32:48]
    g0 = v0 + n * y0
    y1 = shared(g0)
    g1 = b1 + n * y1
    y2 = shared(g1)
    k1 = vd * y1 + down(vw * up(y1))
    m1 = lane_sums(g0 * y1)
    m2 = lane_sums((2.0 * b1 + n * y1) * y1)
    m3 = lane_sums((2.0 * b2 + k1) * y1 + g1 * y2)

    groups, flags, d, w1 = group_flags(parent[...]), category_flags(gam[...]), d_in[...], w1_in[...]
    shares = jnp.concatenate([got[z, 48:64, :] for z in range(8)], axis=0)
    lifted = lifted_categories(shares, flags)
    field = steps(field_in)
    r0 = [field[h] + lifted[h] for h in range(4)]
    br = mixed(r0, d, w1, groups)
    for h in range(4):
        r0_out[h * 128 : (h + 1) * 128, :] = r0[h]
        br_out[h * 128 : (h + 1) * 128, :] = br[h]
    rows = grouped(br, groups)
    m0 = field_product(r0, r0)
    m1 += field_product(r0, br)
    m2 += field_product(br, br)
    m3 += field_product(br, [d * v for v in br]) + lane_sums(w1 * rows * rows)
    moments = jnp.concatenate([m0, m1, m2, m3, jnp.zeros((4, 128), F32)], axis=0)
    for z in range(8):
        out[z, 0:16, :] = y1
        out[z, 16:32, :] = y2
        out[z, 32:40, 0:128] = moments
        out[z, 32:40, 128:256] = jnp.zeros((8, 128), F32)


def fields_kernel(got, r0_in, br_in, d_in, w1_in, parent, gam, out, f_ref, g_ref):
    groups, flags = group_flags(parent[...]), category_flags(gam[...])
    first = lifted_categories(
        jnp.concatenate([got[z, 0:16, :] for z in range(8)], axis=0), flags
    )
    second = lifted_categories(
        jnp.concatenate([got[z, 16:32, :] for z in range(8)], axis=0), flags
    )
    br = steps(br_in)
    field = [br[h] + first[h] for h in range(4)]
    after = mixed(field, d_in[...], w1_in[...], groups)
    for h in range(4):
        f_ref[h * 128 : (h + 1) * 128, :] = field[h]
        g_ref[h * 128 : (h + 1) * 128, :] = after[h] + second[h]
    moments = sum(got[z, 32:40, 0:128] for z in range(8))
    for x in range(4):
        for half in range(2):
            lanes = slice(half * 128, (half + 1) * 128)
            for i, ref in enumerate((r0_in, f_ref, g_ref)):
                pieces = []
                for k in range(4):
                    at = x * 32 + k * 8
                    pieces.append(
                        jnp.concatenate(
                            [ref[h * 128 + at : h * 128 + at + 8, lanes] for h in range(4)], axis=0
                        )
                    )
                pieces = swapped(pieces)
                for g in range(4):
                    out[(half * 4 + g) * 4 + x, i * 32 : (i + 1) * 32, :] = pieces[g]
            for g in range(4):
                out[(half * 4 + g) * 4 + x, 96:104, :] = moments


def finish_kernel(got, x_out, r_out, x_ref, r_ref):
    tile = got[0, 96:104, :]
    for s in range(1, 32):
        tile += got[s, 96:104, :]
    m = jnp.sum(tile, axis=1, keepdims=True)
    m0, m1, m2, m3 = (m[i : i + 1, :] for i in range(4))
    alpha = m0 / m1
    norm = m0 - 2.0 * alpha * m1 + alpha * alpha * m2
    grown = 1.0 + norm / m0
    product = grown * grown * m1 - 2.0 * grown * alpha * m2 + alpha * alpha * m3
    later = norm / product
    on_first, on_second = alpha + later * grown, -later * alpha
    for s in range(32):
        first, second, third = got[s, 0:32, :], got[s, 32:64, :], got[s, 64:96, :]
        x_ref[s * 32 : (s + 1) * 32, :] = on_first * first + on_second * second
        r_ref[s * 32 : (s + 1) * 32, :] = first - on_first * second - on_second * third
    for i in range(8):
        for ref, out in ((x_ref, x_out), (r_ref, r_out)):
            block = ref[pl.ds(i, 128, stride=8), :].T
            for k in range(4):
                out[pl.ds(k * 8 + i, 32, stride=32), :] = block[k * 32 : (k + 1) * 32]


def call(kernel, outs, scratch=()):
    vmem = pl.BlockSpec(memory_space=pltpu.VMEM)
    return lambda *args: pl.pallas_call(
        kernel,
        out_shape=tuple(jax.ShapeDtypeStruct(shape, F32) for shape in outs),
        in_specs=[vmem] * len(args),
        out_specs=(vmem,) * len(outs),
        scratch_shapes=[pltpu.VMEM(shape, F32) for shape in scratch],
    )(*args)


def exchanged(value, axes):
    return lax.all_to_all(value, axes, 0, 0, tiled=True)


def row_of(table, wanted, names):
    hit = table[:, :, None] == wanted[None, None, :]
    return jnp.sum(jnp.where(hit, names[:, None, None], 0), axis=(0, 1), dtype=jnp.int32)[None]


def on_device(b, gi, ac, gc, d, w1, w2, w3, group_table, class_table):
    (sent,) = call(pack_kernel, [(32, 48, 128)], [(1024, 128), (128, 128)])(
        b.reshape(1024, 128),
        d,
        gi.reshape(128, 128),
        w1,
        ac.reshape(32, 128),
        w2.reshape(1, 32),
        gc,
        w3,
    )
    got = exchanged(sent, SPLIT)
    category = jnp.arange(32, dtype=jnp.int32)
    lane = jnp.arange(128, dtype=jnp.int32)
    parent = row_of(group_table, jnp.arange(256, dtype=jnp.int32), category)
    gam = row_of(
        class_table,
        (lane // 32) * 256 + lax.axis_index("z") * 32 + lane % 32,
        (category % 8) * 4 + category // 8,
    )
    sent, field, d_all, w1_all, own = call(
        spread_kernel,
        [(8, 80, 256), (512, 256), (128, 256), (128, 128), (64, 256)],
        [(128, 128), (128, 128)],
    )(got, parent, gam, class_table)
    got = exchanged(sent, "z")
    sent, r0, br = call(middle_kernel, [(8, 40, 256), (512, 256), (512, 256)])(
        got, field, d_all, w1_all, own, parent, gam
    )
    got = exchanged(sent, "z")
    (sent,) = call(fields_kernel, [(32, 104, 128)], [(512, 256), (512, 256)])(
        got, r0, br, d_all, w1_all, parent, gam
    )
    got = exchanged(sent, SPLIT)
    solution_field, residual = call(
        finish_kernel, [(1024, 128)] * 2, [(1024, 128), (1024, 128)]
    )(got)
    return solution_field.reshape(32, 32, 128), residual.reshape(32, 32, 128)


def solution(mesh):
    finer = Mesh(mesh.devices.reshape(4, 2, 4, 8), ("y", "core", "x", "z"))
    return jax.shard_map(
        on_device,
        mesh=finer,
        in_specs=(
            P(REG, PROD, None),
            P(REG, PROD, None),
            P(REG, PROD, None),
            P(REG, None, None),
            P(REG, PROD),
            P(REG, PROD),
            P(REG, PROD),
            P(REG, None),
            P(),
            P(),
        ),
        out_specs=(P(REG, PROD, None), P(REG, PROD, None)),
        check_vma=False,
    )
```

```python
import jax
import jax.numpy as jnp
from jax import lax
from jax.experimental import pallas as pl
from jax.experimental.pallas import tpu as pltpu
from jax.sharding import Mesh
from jax.sharding import PartitionSpec as P

F32 = jnp.float32
BF16 = jnp.bfloat16
REG = ("y", "core")
PROD = ("x", "z")
SPLIT = ("y", "core", "x")
LANES = (((1,), (1,)), ((), ()))


def iota(shape, dim):
    return lax.broadcasted_iota(jnp.int32, shape, dim)


def flag(condition):
    return condition.astype(F32).astype(BF16)


def parts(value):
    high = value.astype(BF16)
    return high, (value - high.astype(F32)).astype(BF16)


def dot(a, b):
    if a.dtype == BF16:
        return sum(jnp.dot(a, p, preferred_element_type=F32) for p in parts(b))
    return sum(jnp.dot(p, b, preferred_element_type=F32) for p in parts(a))


def dot_t(value, flags):
    return sum(lax.dot_general(p, flags, LANES, preferred_element_type=F32) for p in parts(value))


def swapped(pieces):
    group = iota(pieces[0].shape, 1) // 32
    odd, upper = (group & 1) == 1, group >= 2
    a = []
    for i in (0, 2):
        a.append(jnp.where(odd, pltpu.roll(pieces[i + 1], 32, 1), pieces[i]))
        a.append(jnp.where(odd, pieces[i + 1], pltpu.roll(pieces[i], 96, 1)))
    return (
        jnp.where(upper, pltpu.roll(a[2], 64, 1), a[0]),
        jnp.where(upper, pltpu.roll(a[3], 64, 1), a[1]),
        jnp.where(upper, a[2], pltpu.roll(a[0], 64, 1)),
        jnp.where(upper, a[3], pltpu.roll(a[1], 64, 1)),
    )


def group_flags(parent):
    row = iota((128, 256), 0)
    return [flag(row == parent + 32 * h) for h in range(4)]


def category_flags(places):
    row = iota((128, 128), 0)
    return [flag(row == places * 4 + h) for h in range(4)]


def grouped(field, flags):
    return sum(dot_t(field[h], flags[h]) for h in range(4))


def ungrouped(value, flags):
    high, low = parts(value)
    return [
        jnp.dot(high, f, preferred_element_type=F32) + jnp.dot(low, f, preferred_element_type=F32)
        for f in flags
    ]


def mixed(field, precision, group_precision, flags):
    lifted = ungrouped(group_precision * grouped(field, flags), flags)
    return [precision * field[h] + lifted[h] for h in range(4)]


def categories(field, flags):
    return sum(dot(flags[h], field[h]) for h in range(4))


def lifted_categories(value, flags):
    high, low = parts(value)
    dims = (((0,), (0,)), ((), ()))
    return [
        lax.dot_general(f, high, dims, preferred_element_type=F32)
        + lax.dot_general(f, low, dims, preferred_element_type=F32)
        for f in flags
    ]


def steps(ref):
    return [ref[h * 128 : (h + 1) * 128, :] for h in range(4)]


def pack_kernel(b, d, gi, w1, ac, w2, gc, w3, out, turned, turned_small):
    own = lax.axis_index("x") * 8 + lax.axis_index("z")
    for i in range(8):
        block = jnp.concatenate(
            [b[pl.ds(k * 8 + i, 32, stride=32), :] for k in range(4)], axis=0
        )
        turned[pl.ds(i, 128, stride=8), :] = block.T
    d_turned = d[...].T
    d_rows = jnp.concatenate([d_turned[k * 8 : (k + 1) * 8] for k in range(4)], axis=1)
    w1_row = jnp.concatenate([w1[k : k + 1, :] for k in range(4)], axis=1)
    w2_row = jnp.concatenate([w2[...]] * 4, axis=1)
    gi_turned = gi[...].T
    mine = (iota((4, 32, 128), 1) == own).astype(F32)
    corner = jnp.sum(gc[...] * mine, axis=1)
    weight = jnp.sum(jnp.where(iota((4, 32), 1) == own, w3[...], 0.0), axis=1, keepdims=True)
    small = [ac[...], corner * weight, jnp.broadcast_to(weight, (4, 128))]
    small = jnp.concatenate([*small, jnp.zeros((88, 128), F32)], axis=0)
    turned_small[...] = small.T
    values = [turned_small[pl.ds(h, 32, stride=4), :] for h in range(4)]
    a = jnp.concatenate([v[:, 0:32] for v in values], axis=1) * w2_row
    z = jnp.concatenate([v[:, 32:64] for v in values], axis=1)
    for s in range(32):
        out[s, 0:32, :] = turned[s * 32 : (s + 1) * 32, :]
        out[s, 32:40, :] = d_rows
        out[s, 40:44, :] = gi_turned[s * 4 : (s + 1) * 4, :]
        out[s, 44:45, :] = w1_row
        out[s, 45:46, :] = a[s : s + 1, :]
        out[s, 46:47, :] = w2_row
        out[s, 47:48, :] = z[s : s + 1, :]


def spread_kernel(got, parent, gam, table, out, field_out, d_out, w1_out, own_out, g_ref, k_ref):
    for x in range(4):
        for half in range(2):
            lanes = slice(half * 128, (half + 1) * 128)
            pieces = swapped([got[(half * 4 + g) * 4 + x] for g in range(4)])
            for k in range(4):
                piece = pieces[k]
                at = x * 32 + k * 8
                d_out[at : at + 8, lanes] = piece[32:40]
                for h in range(4):
                    field_out[h * 128 + at : h * 128 + at + 8, lanes] = (
                        piece[h * 8 : (h + 1) * 8] * piece[32:40]
                    )
                for i in range(3):
                    own_out[i * 16 + x * 4 + k : i * 16 + x * 4 + k + 1, lanes] = piece[
                        45 + i : 46 + i
                    ]
    for g in range(8):
        pieces = swapped([got[g * 4 + x, 40:48, :] for x in range(4)])
        for k in range(4):
            g_ref[pl.ds(g * 4 + k, 4, stride=32), :] = pieces[k][0:4] * pieces[k][4:5]
            k_ref[pl.ds(g * 4 + k, 4, stride=32), :] = jnp.broadcast_to(
                pieces[k][4:5], (4, 128)
            )
    w1 = k_ref[...].T
    w1_out[...] = w1
    groups = group_flags(parent[...])
    flags = category_flags(gam[...])
    lane = iota((256, 256), 0)
    at = parent[...] // 4 * 32 + parent[...] % 4
    y0 = own_out[0:16, :] + dot(own_out[32:48, :], flag(lane == at))
    own_out[0:16, :] = y0
    d = d_out[...]
    lifted = ungrouped(g_ref[...].T, groups)
    field = [field_out[h * 128 : (h + 1) * 128, :] + lifted[h] for h in range(4)]
    for h in range(4):
        field_out[h * 128 : (h + 1) * 128, :] = field[h]
    totals = [categories(field, flags)]
    for _ in range(2):
        field = mixed(field, d, w1, groups)
        totals.append(categories(field, flags))
    plain = flag(iota((32, 128), 0) == gam[...])
    everywhere = flag(iota((128, 256), 0) % 32 == parent[...])
    members = lax.dot_general(
        jnp.ones((8, 256), BF16), everywhere, LANES, preferred_element_type=F32
    )[0:1]
    lifted_w1 = dot(w1, groups[0])
    small = [dot(plain, v) for v in (d, d * d, d * lifted_w1)]
    row, lane = iota((128, 256), 0), iota((128, 256), 1)
    at = jnp.where(row < 32, row // 4 * 32 + row % 4, -16)
    small.append(
        dot(dot(plain, w1), flag(lane == at + 4))
        + dot(dot(plain, members * w1 * w1), flag(lane == at + 8))
    )
    count = jnp.sum((table[...] >= 0).astype(F32), axis=1, keepdims=True)
    count = jnp.where(iota((32, 1), 0) % 8 == lax.axis_index("z"), count, 0.0)
    for x in range(4):
        size = jnp.sum(count[x * 8 : (x + 1) * 8], axis=0, keepdims=True)
        own_out[48 + x * 4 : 52 + x * 4, :] = jnp.broadcast_to(size, (4, 256))
    for z in range(8):
        for i in range(3):
            out[z, i * 16 : (i + 1) * 16, :] = totals[i][z * 16 : (z + 1) * 16]
        out[z, 48:64, :] = y0
        for i in range(4):
            out[z, 64 + i * 4 : 68 + i * 4, :] = small[i][z * 4 : (z + 1) * 4]


def lane_sums(value):
    rows = jnp.sum(value, axis=0, keepdims=True)
    return sum(rows[:, t * 128 : (t + 1) * 128] for t in range(value.shape[1] // 128))


def field_product(a, b):
    return lane_sums(sum(a[h] * b[h] for h in range(4)))


def middle_kernel(got, field_in, d_in, w1_in, own, parent, gam, out, r0_out, br_out):
    total = sum(got[z, 0:48, :] for z in range(8))
    small = sum(got[z, 64:80, :] for z in range(8))
    v0, v1, v2 = (total[i * 16 : (i + 1) * 16] for i in range(3))

    def repeated(first):
        rows = [
            jnp.broadcast_to(small[first + x : first + x + 1], (4, 256)) for x in range(4)
        ]
        return jnp.concatenate(rows, axis=0)

    vd, vd2, e, vw = (repeated(i * 4) for i in range(4))
    vw2 = pltpu.roll(vw, 252, 1)
    y0, w2, w3, n = (own[i * 16 : (i + 1) * 16, :] for i in range(4))
    at = parent[...] // 4 * 32 + parent[...] % 4 + 4
    places = flag(iota((256, 256), 0) == at)

    def up(value):
        return dot_t(value, places)

    def down(value):
        return dot(value, places)

    def shared(value):
        return w2 * value + down(w3 * up(value))

    sums = up(jnp.concatenate([y0, e * y0], axis=0))
    u0, ue = sums[0:16], sums[16:32]
    lifts = down(jnp.concatenate([u0, vw * u0, ue + vw2 * u0], axis=0))
    b1 = v1 + vd * y0 + lifts[16:32]
    b2 = v2 + vd2 * y0 + e * lifts[0:16] + lifts[32:48]
    g0 = v0 + n * y0
    y1 = shared(g0)
    g1 = b1 + n * y1
    y2 = shared(g1)
    k1 = vd * y1 + down(vw * up(y1))
    m1 = lane_sums(g0 * y1)
    m2 = lane_sums((2.0 * b1 + n * y1) * y1)
    m3 = lane_sums((2.0 * b2 + k1) * y1 + g1 * y2)

    groups, flags, d, w1 = group_flags(parent[...]), category_flags(gam[...]), d_in[...], w1_in[...]
    shares = jnp.concatenate([got[z, 48:64, :] for z in range(8)], axis=0)
    lifted = lifted_categories(shares, flags)
    field = steps(field_in)
    r0 = [field[h] + lifted[h] for h in range(4)]
    br = mixed(r0, d, w1, groups)
    for h in range(4):
        r0_out[h * 128 : (h + 1) * 128, :] = r0[h]
        br_out[h * 128 : (h + 1) * 128, :] = br[h]
    rows = grouped(br, groups)
    m0 = field_product(r0, r0)
    m1 += field_product(r0, br)
    m2 += field_product(br, br)
    m3 += field_product(br, [d * v for v in br]) + lane_sums(w1 * rows * rows)
    moments = jnp.concatenate([m0, m1, m2, m3, jnp.zeros((4, 128), F32)], axis=0)
    for z in range(8):
        out[z, 0:16, :] = y1
        out[z, 16:32, :] = y2
        out[z, 32:40, 0:128] = moments
        out[z, 32:40, 128:256] = jnp.zeros((8, 128), F32)


def fields_kernel(got, r0_in, br_in, d_in, w1_in, parent, gam, out, f_ref, g_ref):
    groups, flags = group_flags(parent[...]), category_flags(gam[...])
    first = lifted_categories(
        jnp.concatenate([got[z, 0:16, :] for z in range(8)], axis=0), flags
    )
    second = lifted_categories(
        jnp.concatenate([got[z, 16:32, :] for z in range(8)], axis=0), flags
    )
    br = steps(br_in)
    field = [br[h] + first[h] for h in range(4)]
    after = mixed(field, d_in[...], w1_in[...], groups)
    for h in range(4):
        f_ref[h * 128 : (h + 1) * 128, :] = field[h]
        g_ref[h * 128 : (h + 1) * 128, :] = after[h] + second[h]
    moments = sum(got[z, 32:40, 0:128] for z in range(8))
    for x in range(4):
        for half in range(2):
            lanes = slice(half * 128, (half + 1) * 128)
            for i, ref in enumerate((r0_in, f_ref, g_ref)):
                pieces = []
                for k in range(4):
                    at = x * 32 + k * 8
                    pieces.append(
                        jnp.concatenate(
                            [ref[h * 128 + at : h * 128 + at + 8, lanes] for h in range(4)], axis=0
                        )
                    )
                pieces = swapped(pieces)
                for g in range(4):
                    out[(half * 4 + g) * 4 + x, i * 32 : (i + 1) * 32, :] = pieces[g]
            for g in range(4):
                out[(half * 4 + g) * 4 + x, 96:104, :] = moments


def finish_kernel(got, x_out, r_out, x_ref, r_ref):
    tile = got[0, 96:104, :]
    for s in range(1, 32):
        tile += got[s, 96:104, :]
    m = jnp.sum(tile, axis=1, keepdims=True)
    m0, m1, m2, m3 = (m[i : i + 1, :] for i in range(4))
    alpha = m0 / m1
    norm = m0 - 2.0 * alpha * m1 + alpha * alpha * m2
    grown = 1.0 + norm / m0
    product = grown * grown * m1 - 2.0 * grown * alpha * m2 + alpha * alpha * m3
    later = norm / product
    on_first, on_second = alpha + later * grown, -later * alpha
    for s in range(32):
        first, second, third = got[s, 0:32, :], got[s, 32:64, :], got[s, 64:96, :]
        x_ref[s * 32 : (s + 1) * 32, :] = on_first * first + on_second * second
        r_ref[s * 32 : (s + 1) * 32, :] = first - on_first * second - on_second * third
    for i in range(8):
        for ref, out in ((x_ref, x_out), (r_ref, r_out)):
            block = ref[pl.ds(i, 128, stride=8), :].T
            for k in range(4):
                out[pl.ds(k * 8 + i, 32, stride=32), :] = block[k * 32 : (k + 1) * 32]


def call(kernel, outs, scratch=(), kept=(), last=False):
    vmem = pl.BlockSpec(memory_space=pltpu.VMEM)
    kind = jax.ShapeDtypeStruct if last else pltpu.VMEM

    def run(*args):
        args = [
            pltpu.with_memory_space_constraint(a, pltpu.VMEM) if i in kept else a
            for i, a in enumerate(args)
        ]
        return pl.pallas_call(
            kernel,
            out_shape=tuple(kind(shape, F32) for shape in outs),
            in_specs=[vmem] * len(args),
            out_specs=(vmem,) * len(outs),
            scratch_shapes=[pltpu.VMEM(shape, F32) for shape in scratch],
            compiler_params=pltpu.CompilerParams(vmem_limit_bytes=(16 if kept else 58) << 20),
        )(*args)

    return run


def exchanged(value, axes):
    return lax.all_to_all(value, axes, 0, 0, tiled=True)


def row_of(table, wanted, names):
    hit = table[:, :, None] == wanted[None, None, :]
    return jnp.sum(jnp.where(hit, names[:, None, None], 0), axis=(0, 1), dtype=jnp.int32)[None]


def on_device(b, gi, ac, gc, d, w1, w2, w3, group_table, class_table):
    (sent,) = call(pack_kernel, [(32, 48, 128)], [(1024, 128), (128, 128)])(
        b.reshape(1024, 128),
        d,
        gi.reshape(128, 128),
        w1,
        ac.reshape(32, 128),
        w2.reshape(1, 32),
        gc,
        w3,
    )
    got = exchanged(sent, SPLIT)
    category = jnp.arange(32, dtype=jnp.int32)
    lane = jnp.arange(128, dtype=jnp.int32)
    parent = row_of(group_table, jnp.arange(256, dtype=jnp.int32), category)
    gam = row_of(
        class_table,
        (lane // 32) * 256 + lax.axis_index("z") * 32 + lane % 32,
        (category % 8) * 4 + category // 8,
    )
    sent, field, d_all, w1_all, own = call(
        spread_kernel,
        [(8, 80, 256), (512, 256), (128, 256), (128, 128), (64, 256)],
        [(128, 128), (128, 128)],
        kept=(0,),
    )(got, parent, gam, class_table)
    got = exchanged(sent, "z")
    sent, r0, br = call(middle_kernel, [(8, 40, 256), (512, 256), (512, 256)], kept=range(5))(
        got, field, d_all, w1_all, own, parent, gam
    )
    got = exchanged(sent, "z")
    (sent,) = call(fields_kernel, [(32, 104, 128)], [(512, 256), (512, 256)], kept=range(5))(
        got, r0, br, d_all, w1_all, parent, gam
    )
    got = exchanged(sent, SPLIT)
    solution_field, residual = call(
        finish_kernel, [(1024, 128)] * 2, [(1024, 128), (1024, 128)], kept=(0,), last=True
    )(got)
    return solution_field.reshape(32, 32, 128), residual.reshape(32, 32, 128)


def solution(mesh):
    finer = Mesh(mesh.devices.reshape(4, 2, 4, 8), ("y", "core", "x", "z"))
    return jax.shard_map(
        on_device,
        mesh=finer,
        in_specs=(
            P(REG, PROD, None),
            P(REG, PROD, None),
            P(REG, PROD, None),
            P(REG, None, None),
            P(REG, PROD),
            P(REG, PROD),
            P(REG, PROD),
            P(REG, None),
            P(),
            P(),
        ),
        out_specs=(P(REG, PROD, None), P(REG, PROD, None)),
        check_vma=False,
    )
```

```python
import jax
import jax.numpy as jnp
from jax import lax
from jax.experimental import pallas as pl
from jax.experimental.pallas import tpu as pltpu
from jax.sharding import Mesh
from jax.sharding import PartitionSpec as P

F32 = jnp.float32
BF16 = jnp.bfloat16
REG = ("y", "core")
PROD = ("x", "far", "near")
SPLIT = ("y", "core", "x", "near")
LANES = (((1,), (1,)), ((), ()))


def iota(shape, dim):
    return lax.broadcasted_iota(jnp.int32, shape, dim)


def flag(condition):
    return condition.astype(F32).astype(BF16)


def parts(value):
    high = value.astype(BF16)
    return high, (value - high.astype(F32)).astype(BF16)


def dot(a, b):
    if a.dtype == BF16:
        return sum(jnp.dot(a, p, preferred_element_type=F32) for p in parts(b))
    return sum(jnp.dot(p, b, preferred_element_type=F32) for p in parts(a))


def dot_t(value, flags):
    return sum(lax.dot_general(p, flags, LANES, preferred_element_type=F32) for p in parts(value))


def swapped(pieces):
    group = iota(pieces[0].shape, 1) // 32
    odd, upper = (group & 1) == 1, group >= 2
    a = []
    for i in (0, 2):
        a.append(jnp.where(odd, pltpu.roll(pieces[i + 1], 32, 1), pieces[i]))
        a.append(jnp.where(odd, pieces[i + 1], pltpu.roll(pieces[i], 96, 1)))
    return (
        jnp.where(upper, pltpu.roll(a[2], 64, 1), a[0]),
        jnp.where(upper, pltpu.roll(a[3], 64, 1), a[1]),
        jnp.where(upper, a[2], pltpu.roll(a[0], 64, 1)),
        jnp.where(upper, a[3], pltpu.roll(a[1], 64, 1)),
    )


def group_flags(parent):
    row = iota((128, 256), 0) % 64
    return [flag(row == parent + 32 * h) for h in range(2)]


def category_flags(places):
    row = iota((64, 256), 0)
    return [flag(row == places * 2 + h) for h in range(2)]


def grouped(field, flags):
    return dot_t(field[0], flags[0]) + dot_t(field[1], flags[1])


def ungrouped(value, flags):
    high = value.astype(BF16).astype(F32)
    both = jnp.where(iota(value.shape, 1) < 64, high, value - high).astype(BF16)
    return [jnp.dot(both, f, preferred_element_type=F32) for f in flags]


def mixed(field, precision, group_precision, flags):
    lifted = ungrouped(group_precision * grouped(field, flags), flags)
    return [precision * field[h] + lifted[h] for h in range(2)]


def categories(field, flags):
    return dot(flags[0], field[0]) + dot(flags[1], field[1])


def lifted_categories(value, places):
    both = jnp.concatenate(parts(value), axis=0)
    lane = (iota((256, 128), 1) % 64).astype(F32)
    flags = [flag(lane == places * 2.0 + h) for h in range(2)]
    return [jnp.dot(f, both, preferred_element_type=F32) for f in flags]


def steps(ref):
    return [ref[h * 256 : (h + 1) * 256, :] for h in range(2)]


def turned_square(ref):
    return jnp.concatenate([ref[:, 0:128].T, ref[:, 128:256].T], axis=0)


def pack_kernel(b, d, gi, w1, ac, w2, gc, w3, out, turned, turned_small):
    own = lax.axis_index("x") * 8 + lax.axis_index("far") * 2 + lax.axis_index("near")
    for i in range(8):
        block = jnp.concatenate(
            [b[pl.ds(k * 8 + i, 32, stride=32), :] for k in range(4)], axis=0
        )
        turned[pl.ds(i, 128, stride=8), :] = block.T
    d_turned = d[...].T
    d_rows = jnp.concatenate([d_turned[k * 8 : (k + 1) * 8] for k in range(4)], axis=1)
    w1_row = jnp.concatenate([w1[k : k + 1, :] for k in range(4)], axis=1)
    w2_row = jnp.concatenate([w2[...]] * 4, axis=1)
    gi_turned = gi[...].T
    mine = (iota((4, 32, 128), 1) == own).astype(F32)
    corner = jnp.sum(gc[...] * mine, axis=1)
    weight = jnp.sum(jnp.where(iota((4, 32), 1) == own, w3[...], 0.0), axis=1, keepdims=True)
    small = [ac[...], corner * weight, jnp.broadcast_to(weight, (4, 128))]
    small = jnp.concatenate([*small, jnp.zeros((88, 128), F32)], axis=0)
    turned_small[...] = small.T
    first, second = (turned_small[pl.ds(h, 64, stride=2), :] for h in range(2))
    corners = jnp.concatenate(
        [first[:, 32:36], second[:, 32:36], first[:, 36:40], jnp.zeros((64, 20), F32)], axis=1
    )
    last = jnp.concatenate([first[:, 0:32], second[:, 0:32], first[:, 0:32], corners], axis=1)
    lane = iota((64, 128), 1)
    last = jnp.where(lane < 96, jnp.where(lane < 64, last * w2_row, w2_row), last)
    for s in range(64):
        at = s * 28
        out[at : at + 16, :] = turned[s * 16 : (s + 1) * 16, :]
        out[at + 16 : at + 24, :] = d_rows
        out[at + 24 : at + 26, :] = gi_turned[s * 2 : (s + 1) * 2, :]
        out[at + 26 : at + 27, :] = w1_row
        out[at + 27 : at + 28, :] = last[s : s + 1, :]


def spread_kernel(
    got, parent, gam, table, out, field_out, d_out, w1_out, own_out, places_out, g_ref, k_ref
):
    for w in range(8):
        for half in range(2):
            lanes = slice(half * 128, (half + 1) * 128)
            first = [((half * 4 + g) * 8 + w) * 28 for g in range(4)]
            pieces = swapped([got[at : at + 28, :] for at in first])
            for k in range(4):
                piece = pieces[k]
                at = w * 32 + k * 8
                d_out[at : at + 8, lanes] = piece[16:24]
                for h in range(2):
                    field_out[h * 256 + at : h * 256 + at + 8, lanes] = (
                        piece[h * 8 : (h + 1) * 8] * piece[16:24]
                    )
            for h in range(2):
                own_out[w * 2 + h : w * 2 + h + 1, lanes] = pieces[h][27:28]
                own_out[16 + w * 2 + h : 17 + w * 2 + h, lanes] = pieces[2][27:28]
                own_out[32 + w * 2 + h : 33 + w * 2 + h, lanes] = pieces[3][27:28]
    for g in range(8):
        for side in range(2):
            lanes = slice(side * 128, (side + 1) * 128)
            first = [(g * 8 + side * 4 + i) * 28 + 24 for i in range(4)]
            pieces = swapped([got[at : at + 4, :] for at in first])
            for k in range(4):
                for copy in range(2):
                    for h in range(2):
                        at = copy * 64 + h * 32 + g * 4 + k
                        g_ref[at : at + 1, lanes] = pieces[k][h : h + 1] * pieces[k][2:3]
                        k_ref[at : at + 1, lanes] = pieces[k][2:3]
    w1 = turned_square(k_ref)
    w1_out[...] = w1
    places_out[...] = jnp.broadcast_to(gam[...].astype(F32), (128, 256)).T
    groups = group_flags(parent[...])
    flags = category_flags(gam[...])
    lane = iota((256, 256), 0)
    at = parent[...] // 4 * 32 + parent[...] % 4
    corner = own_out[32:48, :]
    odd = iota((16, 256), 0) % 2 == 1
    y0 = own_out[0:16, :]
    y0 += jnp.where(odd, dot(corner, flag(lane == at + 4)), dot(corner, flag(lane == at)))
    own_out[0:16, :] = y0
    d = d_out[...]
    lifted = ungrouped(turned_square(g_ref), groups)
    field = [field_out[h * 256 : (h + 1) * 256, :] + lifted[h] for h in range(2)]
    for h in range(2):
        field_out[h * 256 : (h + 1) * 256, :] = field[h]
    totals = [categories(field, flags)]
    for _ in range(2):
        field = mixed(field, d, w1, groups)
        totals.append(categories(field, flags))
    plain = flag(iota((32, 256), 0) == gam[...])
    everywhere = flag(iota((128, 256), 0) % 32 == parent[...])
    members = lax.dot_general(
        jnp.ones((8, 256), BF16), everywhere, LANES, preferred_element_type=F32
    )[0:1]
    lifted_w1 = ungrouped(w1, groups[0:1])[0]
    small = [dot(plain, v) for v in (d, d * d, d * lifted_w1)]
    row, lane = iota((128, 256), 0), iota((128, 256), 1)
    at = jnp.where(row < 32, row // 4 * 32 + row % 4, -16)
    small.append(
        dot(dot(plain, w1), flag(lane == at + 8))
        + dot(dot(plain, members * w1 * w1), flag(lane == at + 12))
    )
    count = jnp.sum((table[...] >= 0).astype(F32), axis=1, keepdims=True)
    count = jnp.where(iota((32, 1), 0) % 8 // 2 == lax.axis_index("far"), count, 0.0)
    for w in range(8):
        part = count[w // 2 * 8 : w // 2 * 8 + 8]
        part = jnp.where(iota((8, 1), 0) % 2 == w % 2, part, 0.0)
        size = jnp.sum(part, axis=0, keepdims=True)
        own_out[48 + w * 2 : 50 + w * 2, :] = jnp.broadcast_to(size, (2, 256))
    for z in range(4):
        for i in range(3):
            out[z, i * 16 : (i + 1) * 16, :] = totals[i][z * 16 : (z + 1) * 16]
        out[z, 48:64, :] = y0
        for i in range(4):
            out[z, 64 + i * 8 : 72 + i * 8, :] = small[i][z * 8 : (z + 1) * 8]


def lane_sums(value):
    rows = jnp.sum(value, axis=0, keepdims=True)
    return sum(rows[:, t * 128 : (t + 1) * 128] for t in range(value.shape[1] // 128))


def field_product(a, b):
    return lane_sums(a[0] * b[0] + a[1] * b[1])


def middle_kernel(got, field_in, d_in, w1_in, own, places_in, parent, out, r0_out, br_out):
    total = sum(got[z, 0:48, :] for z in range(4))
    small = sum(got[z, 64:96, :] for z in range(4))
    v0, v1, v2 = (total[i * 16 : (i + 1) * 16] for i in range(3))

    def repeated(first):
        rows = [
            jnp.broadcast_to(small[first + w : first + w + 1], (2, 256)) for w in range(8)
        ]
        return jnp.concatenate(rows, axis=0)

    vd, vd2, e, vw = (repeated(i * 8) for i in range(4))
    vw2 = pltpu.roll(vw, 252, 1)
    y0, w2, w3, n = (own[i * 16 : (i + 1) * 16, :] for i in range(4))
    at = parent[...] // 4 * 32 + parent[...] % 4 + 8
    places = flag(iota((256, 256), 0) == at)

    def up(value):
        return dot_t(value, places)

    def down(value):
        return dot(value, places)

    def shared(value):
        return w2 * value + down(w3 * up(value))

    sums = up(jnp.concatenate([y0, e * y0], axis=0))
    u0, ue = sums[0:16], sums[16:32]
    lifts = down(jnp.concatenate([u0, vw * u0, ue + vw2 * u0], axis=0))
    b1 = v1 + vd * y0 + lifts[16:32]
    b2 = v2 + vd2 * y0 + e * lifts[0:16] + lifts[32:48]
    g0 = v0 + n * y0
    y1 = shared(g0)
    g1 = b1 + n * y1
    y2 = shared(g1)
    k1 = vd * y1 + down(vw * up(y1))
    m1 = lane_sums(g0 * y1)
    m2 = lane_sums((2.0 * b1 + n * y1) * y1)
    m3 = lane_sums((2.0 * b2 + k1) * y1 + g1 * y2)

    groups, d, w1 = group_flags(parent[...]), d_in[...], w1_in[...]
    shares = jnp.concatenate([got[z, 48:64, :] for z in range(4)], axis=0)
    lifted = lifted_categories(shares, places_in[...])
    field = steps(field_in)
    r0 = [field[h] + lifted[h] for h in range(2)]
    br = mixed(r0, d, w1, groups)
    for h in range(2):
        r0_out[h * 256 : (h + 1) * 256, :] = r0[h]
        br_out[h * 256 : (h + 1) * 256, :] = br[h]
    rows = grouped(br, groups)
    m0 = field_product(r0, r0)
    m1 += field_product(r0, br)
    m2 += field_product(br, br)
    m3 += field_product(br, [d * v for v in br]) + 0.5 * lane_sums(w1 * rows * rows)
    moments = jnp.concatenate([m0, m1, m2, m3, jnp.zeros((4, 128), F32)], axis=0)
    moments = jnp.sum(moments, axis=1, keepdims=True)
    at_lane = iota((8, 128), 0) == iota((8, 128), 1)
    moments = jnp.sum(jnp.where(at_lane, moments, 0.0), axis=0, keepdims=True)
    for z in range(4):
        at = z * 66
        for t in range(2):
            out[at + t * 16 : at + (t + 1) * 16, :] = y1[:, t * 128 : (t + 1) * 128]
            out[at + 32 + t * 16 : at + 48 + t * 16, :] = y2[:, t * 128 : (t + 1) * 128]
        out[at + 64 : at + 66, :] = jnp.concatenate([moments] * 2, axis=0)


def fields_kernel(got, r0_in, br_in, d_in, w1_in, places_in, parent, out, f_ref, g_ref):
    groups, category = group_flags(parent[...]), places_in[...]

    def shares(first):
        tiles = [
            jnp.concatenate([got[z * 66 + at : z * 66 + at + 16, :] for z in range(4)], axis=0)
            for at in (first, first + 16)
        ]
        return jnp.concatenate(tiles, axis=1)

    first = lifted_categories(shares(0), category)
    second = lifted_categories(shares(32), category)
    br = steps(br_in)
    field = [br[h] + first[h] for h in range(2)]
    after = mixed(field, d_in[...], w1_in[...], groups)
    for h in range(2):
        f_ref[h * 256 : (h + 1) * 256, :] = field[h]
        g_ref[h * 256 : (h + 1) * 256, :] = after[h] + second[h]
    moments = sum(got[z * 66 + 64 : z * 66 + 65, :] for z in range(4))
    for w in range(8):
        for half in range(2):
            lanes = slice(half * 128, (half + 1) * 128)
            for i, ref in enumerate((r0_in, f_ref, g_ref)):
                pieces = []
                for k in range(4):
                    at = w * 32 + k * 8
                    pieces.append(
                        jnp.concatenate(
                            [ref[h * 256 + at : h * 256 + at + 8, lanes] for h in range(2)], axis=0
                        )
                    )
                pieces = swapped(pieces)
                for g in range(4):
                    at = ((half * 4 + g) * 8 + w) * 49 + i * 16
                    out[at : at + 16, :] = pieces[g]
            for g in range(4):
                at = ((half * 4 + g) * 8 + w) * 49 + 48
                out[at : at + 1, :] = moments


def finish_kernel(got, x_out, r_out, x_ref, r_ref):
    m = got[48:49, :]
    for s in range(1, 64):
        m += got[s * 49 + 48 : s * 49 + 49, :]
    m0, m1, m2, m3 = (m[:, i : i + 1] for i in range(4))
    alpha = m0 / m1
    norm = m0 - 2.0 * alpha * m1 + alpha * alpha * m2
    grown = 1.0 + norm / m0
    product = grown * grown * m1 - 2.0 * grown * alpha * m2 + alpha * alpha * m3
    later = norm / product
    on_first, on_second = alpha + later * grown, -later * alpha
    for s in range(64):
        first, second, third = (got[s * 49 + i * 16 : s * 49 + i * 16 + 16, :] for i in range(3))
        x_ref[s * 16 : (s + 1) * 16, :] = on_first * first + on_second * second
        r_ref[s * 16 : (s + 1) * 16, :] = first - on_first * second - on_second * third
    for i in range(8):
        for ref, out in ((x_ref, x_out), (r_ref, r_out)):
            block = ref[pl.ds(i, 128, stride=8), :].T
            for k in range(4):
                out[pl.ds(k * 8 + i, 32, stride=32), :] = block[k * 32 : (k + 1) * 32]


def call(kernel, outs, scratch=(), kept=(), last=False):
    vmem = pl.BlockSpec(memory_space=pltpu.VMEM)
    kind = jax.ShapeDtypeStruct if last else pltpu.VMEM

    def run(*args):
        args = [
            pltpu.with_memory_space_constraint(a, pltpu.VMEM) if i in kept else a
            for i, a in enumerate(args)
        ]
        return pl.pallas_call(
            kernel,
            out_shape=tuple(kind(shape, F32) for shape in outs),
            in_specs=[vmem] * len(args),
            out_specs=(vmem,) * len(outs),
            scratch_shapes=[pltpu.VMEM(shape, F32) for shape in scratch],
            compiler_params=pltpu.CompilerParams(vmem_limit_bytes=(16 if kept else 58) << 20),
        )(*args)

    return run


def exchanged(value, axes, blocks, tile):
    shape = value.shape
    value = value.reshape(blocks, -1, tile, shape[-1])
    return lax.all_to_all(value, axes, 0, 0, tiled=True).reshape(shape)


def row_of(table, wanted, names):
    hit = table[:, :, None] == wanted[None, None, :]
    return jnp.sum(jnp.where(hit, names[:, None, None], 0), axis=(0, 1), dtype=jnp.int32)[None]


def on_device(b, gi, ac, gc, d, w1, w2, w3, group_table, class_table):
    (sent,) = call(pack_kernel, [(64 * 28, 128)], [(1024, 128), (128, 128)])(
        b.reshape(1024, 128),
        d,
        gi.reshape(128, 128),
        w1,
        ac.reshape(32, 128),
        w2.reshape(1, 32),
        gc,
        w3,
    )
    got = exchanged(sent, SPLIT, 64, 4)
    category = jnp.arange(32, dtype=jnp.int32)
    lane = jnp.arange(256, dtype=jnp.int32)
    parent = row_of(group_table, lane, category)
    product = lane // 64 * 256 + lax.axis_index("far") * 64 + lane % 64
    place = category % 8 // 2 * 8 + category // 8 * 2 + category % 2
    gam = row_of(class_table, product, place)
    sent, field, d_all, w1_all, own, places = call(
        spread_kernel,
        [(4, 96, 256), (512, 256), (256, 256), (256, 128), (64, 256), (256, 128)],
        [(128, 256), (128, 256)],
        kept=(0,),
    )(got, parent, gam, class_table)
    got = exchanged(sent, "far", 4, 8)
    sent, r0, br = call(middle_kernel, [(4 * 66, 128), (512, 256), (512, 256)], kept=range(6))(
        got, field, d_all, w1_all, own, places, parent
    )
    got = exchanged(sent, "far", 4, 2)
    (sent,) = call(fields_kernel, [(64 * 49, 128)], [(512, 256), (512, 256)], kept=range(6))(
        got, r0, br, d_all, w1_all, places, parent
    )
    got = exchanged(sent, SPLIT, 64, 1)
    solution_field, residual = call(
        finish_kernel, [(1024, 128)] * 2, [(1024, 128), (1024, 128)], kept=(0,), last=True
    )(got)
    return solution_field.reshape(32, 32, 128), residual.reshape(32, 32, 128)


def solution(mesh):
    finer = Mesh(
        mesh.devices.reshape(4, 2, 4, 4, 2), ("y", "core", "x", "far", "near")
    )
    return jax.shard_map(
        on_device,
        mesh=finer,
        in_specs=(
            P(REG, PROD, None),
            P(REG, PROD, None),
            P(REG, PROD, None),
            P(REG, None, None),
            P(REG, PROD),
            P(REG, PROD),
            P(REG, PROD),
            P(REG, None),
            P(),
            P(),
        ),
        out_specs=(P(REG, PROD, None), P(REG, PROD, None)),
        check_vma=False,
    )
```

```python
import jax
import jax.numpy as jnp
from jax import lax
from jax.experimental import pallas as pl
from jax.experimental.pallas import tpu as pltpu
from jax.sharding import Mesh
from jax.sharding import PartitionSpec as P

F32 = jnp.float32
BF16 = jnp.bfloat16
REG = ("y", "core")
PROD = ("x", "far", "near")
SPLIT = ("y", "core", "x", "near")
LANES = (((1,), (1,)), ((), ()))


def iota(shape, dim):
    return lax.broadcasted_iota(jnp.int32, shape, dim)


def flag(condition):
    return condition.astype(F32).astype(BF16)


def parts(value):
    high = value.astype(BF16)
    return high, (value - high.astype(F32)).astype(BF16)


def dot(a, b):
    if a.dtype == BF16:
        return sum(jnp.dot(a, p, preferred_element_type=F32) for p in parts(b))
    return sum(jnp.dot(p, b, preferred_element_type=F32) for p in parts(a))


def swapped(pieces):
    group = iota(pieces[0].shape, 1) // 32
    odd, upper = (group & 1) == 1, group >= 2
    a = []
    for i in (0, 2):
        a.append(jnp.where(odd, pltpu.roll(pieces[i + 1], 32, 1), pieces[i]))
        a.append(jnp.where(odd, pieces[i + 1], pltpu.roll(pieces[i], 96, 1)))
    low, high = [], []
    for i in range(2):
        moved = pltpu.roll(jnp.where(upper, a[i], a[i + 2]), 64, 1)
        low.append(jnp.where(upper, moved, a[i]))
        high.append(jnp.where(upper, a[i + 2], moved))
    return low + high


def group_flags(parent):
    row = iota((128, 256), 0) % 64
    return [flag(row == parent + 32 * h) for h in range(2)]


def category_flags(places):
    row = iota((64, 256), 0)
    return [flag(row == places * 2 + h) for h in range(2)]


def ungrouped(value, flags):
    high = value.astype(BF16).astype(F32)
    both = jnp.where(iota(value.shape, 1) < 64, high, value - high).astype(BF16)
    return [jnp.dot(both, f, preferred_element_type=F32) for f in flags]


def same_parent(parent, column):
    column = jnp.concatenate([column, column], axis=1)
    return flag(column == parent.astype(F32))


def mixed(field, precision, group_precision, same):
    return [precision * v + group_precision * dot(v, same) for v in field]


def categories(field, flags):
    return dot(flags[0], field[0]) + dot(flags[1], field[1])


def lifted_categories(value, places):
    both = jnp.concatenate(parts(value), axis=0)
    lane = (iota((256, 128), 1) % 64).astype(F32)
    flags = [flag(lane == places * 2.0 + h) for h in range(2)]
    return [jnp.dot(f, both, preferred_element_type=F32) for f in flags]


def steps(ref):
    return [ref[h * 256 : (h + 1) * 256, :] for h in range(2)]


def turned_square(ref):
    return jnp.concatenate([ref[:, 0:128].T, ref[:, 128:256].T], axis=0)


def pack_kernel(b, d, gi, w1, ac, w2, gc, w3, out, turned, turned_small):
    own = lax.axis_index("x") * 8 + lax.axis_index("far") * 2 + lax.axis_index("near")
    for i in range(8):
        block = jnp.concatenate(
            [b[pl.ds(k * 8 + i, 32, stride=32), :] for k in range(4)], axis=0
        )
        turned[pl.ds(i, 128, stride=8), :] = block.T
    d_turned = d[...].T
    d_rows = jnp.concatenate([d_turned[k * 8 : (k + 1) * 8] for k in range(4)], axis=1)
    w1_row = jnp.concatenate([w1[k : k + 1, :] for k in range(4)], axis=1)
    w2_row = jnp.concatenate([w2[...]] * 4, axis=1)
    gi_turned = gi[...].T
    mine = (iota((4, 32, 128), 1) == own).astype(F32)
    corner = jnp.sum(gc[...] * mine, axis=1)
    weight = jnp.sum(jnp.where(iota((4, 32), 1) == own, w3[...], 0.0), axis=1, keepdims=True)
    small = [ac[...], corner * weight, jnp.broadcast_to(weight, (4, 128))]
    small = jnp.concatenate([*small, jnp.zeros((88, 128), F32)], axis=0)
    turned_small[...] = small.T
    first, second = (turned_small[pl.ds(h, 64, stride=2), :] for h in range(2))
    corners = jnp.concatenate(
        [first[:, 32:36], second[:, 32:36], first[:, 36:40], jnp.zeros((64, 20), F32)], axis=1
    )
    last = jnp.concatenate([first[:, 0:32], second[:, 0:32], first[:, 0:32], corners], axis=1)
    lane = iota((64, 128), 1)
    last = jnp.where(lane < 96, jnp.where(lane < 64, last * w2_row, w2_row), last)
    for s in range(64):
        at = s * 28
        out[at : at + 16, :] = turned[s * 16 : (s + 1) * 16, :]
        out[at + 16 : at + 24, :] = d_rows
        out[at + 24 : at + 26, :] = gi_turned[s * 2 : (s + 1) * 2, :]
        out[at + 26 : at + 27, :] = w1_row
        out[at + 27 : at + 28, :] = last[s : s + 1, :]


def spread_kernel(
    got, parent, gam, table, out, field_out, d_out, w1_out, own_out, places_out, column_out,
    g_ref, k_ref,
):
    for w in range(8):
        for half in range(2):
            lanes = slice(half * 128, (half + 1) * 128)
            first = [((half * 4 + g) * 8 + w) * 28 for g in range(4)]
            pieces = swapped([got[at : at + 28, :] for at in first])
            for k in range(4):
                piece = pieces[k]
                at = w * 32 + k * 8
                d_out[at : at + 8, lanes] = piece[16:24]
                for h in range(2):
                    field_out[h * 256 + at : h * 256 + at + 8, lanes] = (
                        piece[h * 8 : (h + 1) * 8] * piece[16:24]
                    )
            for h in range(2):
                own_out[w * 2 + h : w * 2 + h + 1, lanes] = pieces[h][27:28]
                own_out[16 + w * 2 + h : 17 + w * 2 + h, lanes] = pieces[2][27:28]
                own_out[32 + w * 2 + h : 33 + w * 2 + h, lanes] = pieces[3][27:28]
    for g in range(8):
        for side in range(2):
            lanes = slice(side * 128, (side + 1) * 128)
            first = [(g * 8 + side * 4 + i) * 28 + 24 for i in range(4)]
            pieces = swapped([got[at : at + 4, :] for at in first])
            for k in range(4):
                for h in range(2):
                    at = h * 32 + g * 4 + k
                    g_ref[at : at + 1, lanes] = pieces[k][h : h + 1] * pieces[k][2:3]
                k_ref[g * 4 + k : g * 4 + k + 1, lanes] = pieces[k][2:3]
    g_ref[64:128, :] = g_ref[0:64, :]
    for i in range(1, 4):
        k_ref[i * 32 : (i + 1) * 32, :] = k_ref[0:32, :]
    w1 = turned_square(k_ref)
    column = jnp.broadcast_to(parent[...].astype(F32), (128, 256)).T
    column_out[...] = column
    same = same_parent(parent[...], column)
    places_out[...] = jnp.broadcast_to(gam[...].astype(F32), (128, 256)).T
    groups = group_flags(parent[...])
    flags = category_flags(gam[...])
    lane = iota((256, 256), 0)
    at = parent[...] // 4 * 32 + parent[...] % 4
    corner = own_out[32:48, :]
    odd = iota((16, 256), 0) % 2 == 1
    y0 = own_out[0:16, :]
    y0 += jnp.where(odd, dot(corner, flag(lane == at + 4)), dot(corner, flag(lane == at)))
    own_out[0:16, :] = y0
    own_out[32:48, :] = dot(corner, flag(lane == at + 8))
    d = d_out[...]
    w1_lifted = ungrouped(w1, groups[0:1])[0]
    w1_out[...] = w1_lifted
    lifted = ungrouped(turned_square(g_ref), groups)
    field = [field_out[h * 256 : (h + 1) * 256, :] + lifted[h] for h in range(2)]
    for h in range(2):
        field_out[h * 256 : (h + 1) * 256, :] = field[h]
    totals = [categories(field, flags)]
    for _ in range(2):
        field = mixed(field, d, w1_lifted, same)
        totals.append(categories(field, flags))
    plain = flag(iota((32, 256), 0) == gam[...])
    everywhere = flag(iota((128, 256), 0) % 32 == parent[...])
    members = lax.dot_general(
        jnp.ones((8, 256), BF16), everywhere, LANES, preferred_element_type=F32
    )[0:1]
    small = [dot(plain, v) for v in (d, d * d, d * w1_lifted)]
    row, lane = iota((128, 256), 0), iota((128, 256), 1)
    at = jnp.where(row < 32, row // 4 * 32 + row % 4, -16)
    small.append(
        dot(dot(plain, w1), flag(lane == at + 8))
        + dot(dot(plain, members * w1 * w1), flag(lane == at + 12))
    )
    count = jnp.sum((table[...] >= 0).astype(F32), axis=1, keepdims=True)
    count = jnp.where(iota((32, 1), 0) % 8 // 2 == lax.axis_index("far"), count, 0.0)
    for w in range(8):
        part = count[w // 2 * 8 : w // 2 * 8 + 8]
        part = jnp.where(iota((8, 1), 0) % 2 == w % 2, part, 0.0)
        size = jnp.sum(part, axis=0, keepdims=True)
        own_out[48 + w * 2 : 50 + w * 2, :] = jnp.broadcast_to(size, (2, 256))
    for z in range(4):
        for i in range(3):
            out[z, i * 16 : (i + 1) * 16, :] = totals[i][z * 16 : (z + 1) * 16]
        out[z, 48:64, :] = y0
        for i in range(4):
            out[z, 64 + i * 8 : 72 + i * 8, :] = small[i][z * 8 : (z + 1) * 8]


def lane_sums(value):
    rows = jnp.sum(value, axis=0, keepdims=True)
    return sum(rows[:, t * 128 : (t + 1) * 128] for t in range(value.shape[1] // 128))


def field_product(a, b):
    return lane_sums(a[0] * b[0] + a[1] * b[1])


def middle_kernel(
    got, field_in, d_in, w1_in, own, places_in, column, parent, out, r0_out, br_out
):
    total = sum(got[z, 0:48, :] for z in range(4))
    small = sum(got[z, 64:96, :] for z in range(4))
    v0, v1, v2 = (total[i * 16 : (i + 1) * 16] for i in range(3))

    def repeated(value):
        return jnp.concatenate(
            [jnp.broadcast_to(value[w : w + 1], (2, 256)) for w in range(8)], axis=0
        )

    y0, w2, w3, n = (own[i * 16 : (i + 1) * 16, :] for i in range(4))
    lane = iota((256, 256), 0)
    at = parent[...] // 4 * 32 + parent[...] % 4
    vd, vd2, e = (repeated(small[i * 8 : (i + 1) * 8]) for i in range(3))
    vw, vw2 = (repeated(dot(small[24:32], flag(lane == at + i))) for i in (8, 12))
    same = same_parent(parent[...], column[...])
    g0 = v0 + n * y0
    shared = dot(jnp.concatenate([y0, e * y0, g0], axis=0), same)
    b1 = v1 + vd * y0 + vw * shared[0:16]
    b2 = v2 + vd2 * y0 + (e + vw2) * shared[0:16] + shared[16:32]
    y1 = w2 * g0 + w3 * shared[32:48]
    g1 = b1 + n * y1
    shared = dot(jnp.concatenate([y1, g1], axis=0), same)
    k1 = vd * y1 + vw * shared[0:16]
    y2 = w2 * g1 + w3 * shared[16:32]
    m1 = lane_sums(g0 * y1)
    m2 = lane_sums((2.0 * b1 + n * y1) * y1)
    m3 = lane_sums((2.0 * b2 + k1) * y1 + g1 * y2)

    d, w1 = d_in[...], w1_in[...]
    shares = jnp.concatenate([got[z, 48:64, :] for z in range(4)], axis=0)
    lifted = lifted_categories(shares, places_in[...])
    field = steps(field_in)
    r0 = [field[h] + lifted[h] for h in range(2)]
    br = mixed(r0, d, w1, same)
    for h in range(2):
        r0_out[h * 256 : (h + 1) * 256, :] = r0[h]
        br_out[h * 256 : (h + 1) * 256, :] = br[h]
    m0 = field_product(r0, r0)
    m1 += field_product(r0, br)
    m2 += field_product(br, br)
    m3 += field_product(br, mixed(br, d, w1, same))
    moments = jnp.concatenate([m0, m1, m2, m3, jnp.zeros((4, 128), F32)], axis=0)
    moments = jnp.sum(moments, axis=1, keepdims=True)
    at_lane = iota((8, 128), 0) == iota((8, 128), 1)
    moments = jnp.sum(jnp.where(at_lane, moments, 0.0), axis=0, keepdims=True)
    for z in range(4):
        at = z * 66
        for t in range(2):
            out[at + t * 16 : at + (t + 1) * 16, :] = y1[:, t * 128 : (t + 1) * 128]
            out[at + 32 + t * 16 : at + 48 + t * 16, :] = y2[:, t * 128 : (t + 1) * 128]
        out[at + 64 : at + 66, :] = jnp.concatenate([moments] * 2, axis=0)


def fields_kernel(got, r0_in, br_in, d_in, w1_in, places_in, column, parent, out, f_ref, g_ref):
    same, category = same_parent(parent[...], column[...]), places_in[...]

    def shares(first):
        tiles = [
            jnp.concatenate([got[z * 66 + at : z * 66 + at + 16, :] for z in range(4)], axis=0)
            for at in (first, first + 16)
        ]
        return jnp.concatenate(tiles, axis=1)

    first = lifted_categories(shares(0), category)
    second = lifted_categories(shares(32), category)
    br = steps(br_in)
    field = [br[h] + first[h] for h in range(2)]
    after = mixed(field, d_in[...], w1_in[...], same)
    for h in range(2):
        f_ref[h * 256 : (h + 1) * 256, :] = field[h]
        g_ref[h * 256 : (h + 1) * 256, :] = after[h] + second[h]
    moments = sum(got[z * 66 + 64 : z * 66 + 65, :] for z in range(4))
    for w in range(8):
        for half in range(2):
            lanes = slice(half * 128, (half + 1) * 128)
            for i, ref in enumerate((r0_in, f_ref, g_ref)):
                pieces = []
                for k in range(4):
                    at = w * 32 + k * 8
                    pieces.append(
                        jnp.concatenate(
                            [ref[h * 256 + at : h * 256 + at + 8, lanes] for h in range(2)], axis=0
                        )
                    )
                pieces = swapped(pieces)
                for g in range(4):
                    at = ((half * 4 + g) * 8 + w) * 49 + i * 16
                    out[at : at + 16, :] = pieces[g]
            for g in range(4):
                at = ((half * 4 + g) * 8 + w) * 49 + 48
                out[at : at + 1, :] = moments


def finish_kernel(got, x_out, r_out, x_ref, r_ref, turned, sems):
    sums = [
        sum(got[s * 49 + 48 : s * 49 + 49, :] for s in range(i, 64, 8)) for i in range(8)
    ]
    m = sum(sums)
    m0, m1, m2, m3 = (m[:, i : i + 1] for i in range(4))
    alpha = m0 / m1
    norm = m0 - 2.0 * alpha * m1 + alpha * alpha * m2
    grown = 1.0 + norm / m0
    product = grown * grown * m1 - 2.0 * grown * alpha * m2 + alpha * alpha * m3
    later = norm / product
    on_first, on_second = alpha + later * grown, -later * alpha
    for s in range(64):
        first, second, third = (got[s * 49 + i * 16 : s * 49 + i * 16 + 16, :] for i in range(3))
        x_ref[s * 16 : (s + 1) * 16, :] = on_first * first + on_second * second
        r_ref[s * 16 : (s + 1) * 16, :] = first - on_first * second - on_second * third
    copies = []
    for j, (ref, out) in enumerate(((x_ref, x_out), (r_ref, r_out))):
        for i in range(8):
            block = ref[pl.ds(i, 128, stride=8), :].T
            for k in range(4):
                turned[pl.ds(j * 1024 + k * 8 + i, 32, stride=32), :] = block[
                    k * 32 : (k + 1) * 32
                ]
        copy = pltpu.make_async_copy(turned.at[pl.ds(j * 1024, 1024), :], out, sems.at[j])
        copy.start()
        copies.append(copy)
    for copy in copies:
        copy.wait()


def call(kernel, outs, scratch=(), kept=(), last=False):
    vmem = pl.BlockSpec(memory_space=pltpu.VMEM)
    kind = jax.ShapeDtypeStruct if last else pltpu.VMEM

    def run(*args):
        args = [
            pltpu.with_memory_space_constraint(a, pltpu.VMEM) if i in kept else a
            for i, a in enumerate(args)
        ]
        return pl.pallas_call(
            kernel,
            out_shape=tuple(kind(shape, F32) for shape in outs),
            in_specs=[vmem] * len(args),
            out_specs=(pl.BlockSpec(memory_space=pl.ANY) if last else vmem,) * len(outs),
            scratch_shapes=[pltpu.VMEM(shape, F32) for shape in scratch]
            + [pltpu.SemaphoreType.DMA((2,))] * last,
            compiler_params=pltpu.CompilerParams(vmem_limit_bytes=(16 if kept else 58) << 20),
        )(*args)

    return run


def exchanged(value, axes, blocks, tile):
    shape = value.shape
    value = value.reshape(blocks, -1, tile, shape[-1])
    return lax.all_to_all(value, axes, 0, 0, tiled=True).reshape(shape)


def row_of(table, wanted, names):
    hit = table[:, :, None] == wanted[None, None, :]
    return jnp.sum(jnp.where(hit, names[:, None, None], 0), axis=(0, 1), dtype=jnp.int32)[None]


def on_device(b, gi, ac, gc, d, w1, w2, w3, group_table, class_table):
    (sent,) = call(pack_kernel, [(64 * 28, 128)], [(1024, 128), (128, 128)])(
        b.reshape(1024, 128),
        d,
        gi.reshape(128, 128),
        w1,
        ac.reshape(32, 128),
        w2.reshape(1, 32),
        gc,
        w3,
    )
    got = exchanged(sent, SPLIT, 64, 4)
    category = jnp.arange(32, dtype=jnp.int32)
    lane = jnp.arange(256, dtype=jnp.int32)
    parent = row_of(group_table, lane, category)
    product = lane // 64 * 256 + lax.axis_index("far") * 64 + lane % 64
    place = category % 8 // 2 * 8 + category // 8 * 2 + category % 2
    gam = row_of(class_table, product, place)
    sent, field, d_all, w1_all, own, places, column = call(
        spread_kernel,
        [(4, 96, 256), (512, 256), (256, 256), (256, 256), (64, 256), (256, 128), (256, 128)],
        [(128, 256), (128, 256)],
        kept=(0,),
    )(got, parent, gam, class_table)
    got = exchanged(sent, "far", 4, 8)
    sent, r0, br = call(middle_kernel, [(4 * 66, 128), (512, 256), (512, 256)], kept=range(7))(
        got, field, d_all, w1_all, own, places, column, parent
    )
    got = exchanged(sent, "far", 4, 2)
    (sent,) = call(fields_kernel, [(64 * 49, 128)], [(512, 256), (512, 256)], kept=range(7))(
        got, r0, br, d_all, w1_all, places, column, parent
    )
    got = exchanged(sent, SPLIT, 64, 1)
    solution_field, residual = call(
        finish_kernel,
        [(1024, 128)] * 2,
        [(1024, 128), (1024, 128), (2048, 128)],
        kept=(0,),
        last=True,
    )(got)
    return solution_field.reshape(32, 32, 128), residual.reshape(32, 32, 128)


def solution(mesh):
    finer = Mesh(
        mesh.devices.reshape(4, 2, 4, 4, 2), ("y", "core", "x", "far", "near")
    )
    return jax.shard_map(
        on_device,
        mesh=finer,
        in_specs=(
            P(REG, PROD, None),
            P(REG, PROD, None),
            P(REG, PROD, None),
            P(REG, None, None),
            P(REG, PROD),
            P(REG, PROD),
            P(REG, PROD),
            P(REG, None),
            P(),
            P(),
        ),
        out_specs=(P(REG, PROD, None), P(REG, PROD, None)),
        check_vma=False,
    )
```

```python
import jax
import jax.numpy as jnp
from jax import lax
from jax.experimental import pallas as pl
from jax.experimental.pallas import tpu as pltpu
from jax.sharding import Mesh
from jax.sharding import PartitionSpec as P

F32 = jnp.float32
BF16 = jnp.bfloat16
REG = ("y", "core")
PROD = ("x", "far", "near")
SPLIT = ("y", "core", "x", "near")
LANES = (((1,), (1,)), ((), ()))


def iota(shape, dim):
    return lax.broadcasted_iota(jnp.int32, shape, dim)


def flag(condition):
    return condition.astype(F32).astype(BF16)


def parts(value):
    high = value.astype(BF16)
    return high, (value - high.astype(F32)).astype(BF16)


def dot(a, b):
    if a.dtype == BF16:
        a, b = jnp.concatenate([a, a], axis=1), jnp.concatenate(parts(b), axis=0)
    else:
        a, b = jnp.concatenate(parts(a), axis=1), jnp.concatenate([b, b], axis=0)
    return jnp.dot(a, b, preferred_element_type=F32)


def swapped(pieces):
    group = iota(pieces[0].shape, 1) // 32
    odd, upper = (group & 1) == 1, group >= 2
    a = []
    for i in (0, 2):
        a.append(jnp.where(odd, pltpu.roll(pieces[i + 1], 32, 1), pieces[i]))
        a.append(jnp.where(odd, pieces[i + 1], pltpu.roll(pieces[i], 96, 1)))
    low, high = [], []
    for i in range(2):
        moved = pltpu.roll(jnp.where(upper, a[i], a[i + 2]), 64, 1)
        low.append(jnp.where(upper, moved, a[i]))
        high.append(jnp.where(upper, a[i + 2], moved))
    return low + high


def group_flags(parent):
    row = iota((128, 256), 0) % 64
    return [flag(row == parent + 32 * h) for h in range(2)]


def category_flags(places):
    row = iota((64, 256), 0)
    return [flag(row == places * 2 + h) for h in range(2)]


def ungrouped(value, flags):
    high = value.astype(BF16).astype(F32)
    both = jnp.where(iota(value.shape, 1) < 64, high, value - high).astype(BF16)
    return [jnp.dot(both, f, preferred_element_type=F32) for f in flags]


def same_parent(parent, column):
    column = jnp.concatenate([column, column], axis=1)
    return flag(column == parent.astype(F32))


def mixed(field, precision, group_precision, same):
    return [precision * v + group_precision * dot(v, same) for v in field]


def categories(field, flags):
    return dot(flags[0], field[0]) + dot(flags[1], field[1])


def lifted_categories(value, places):
    both = jnp.concatenate(parts(value), axis=0)
    lane = (iota((256, 128), 1) % 64).astype(F32)
    flags = [flag(lane == places * 2.0 + h) for h in range(2)]
    return [jnp.dot(f, both, preferred_element_type=F32) for f in flags]


def steps(ref):
    return [ref[h * 256 : (h + 1) * 256, :] for h in range(2)]


def turned_square(ref):
    return jnp.concatenate([ref[:, 0:128].T, ref[:, 128:256].T], axis=0)


def pack_kernel(b, d, gi, w1, ac, w2, gc, w3, out, turned, turned_small):
    own = lax.axis_index("x") * 8 + lax.axis_index("far") * 2 + lax.axis_index("near")
    for i in range(8):
        block = jnp.concatenate(
            [b[pl.ds(k * 8 + i, 32, stride=32), :] for k in range(4)], axis=0
        )
        turned[pl.ds(i, 128, stride=8), :] = block.T
    d_turned = d[...].T
    d_rows = jnp.concatenate([d_turned[k * 8 : (k + 1) * 8] for k in range(4)], axis=1)
    w1_row = jnp.concatenate([w1[k : k + 1, :] for k in range(4)], axis=1)
    w2_row = jnp.concatenate([w2[...]] * 4, axis=1)
    gi_turned = gi[...].T
    mine = (iota((4, 32, 128), 1) == own).astype(F32)
    corner = jnp.sum(gc[...] * mine, axis=1)
    weight = jnp.sum(jnp.where(iota((4, 32), 1) == own, w3[...], 0.0), axis=1, keepdims=True)
    small = [ac[...], corner * weight, jnp.broadcast_to(weight, (4, 128))]
    small = jnp.concatenate([*small, jnp.zeros((88, 128), F32)], axis=0)
    turned_small[...] = small.T
    first, second = (turned_small[pl.ds(h, 64, stride=2), :] for h in range(2))
    corners = jnp.concatenate(
        [first[:, 32:36], second[:, 32:36], first[:, 36:40], jnp.zeros((64, 20), F32)], axis=1
    )
    last = jnp.concatenate([first[:, 0:32], second[:, 0:32], first[:, 0:32], corners], axis=1)
    lane = iota((64, 128), 1)
    last = jnp.where(lane < 96, jnp.where(lane < 64, last * w2_row, w2_row), last)
    for s in range(64):
        at = s * 28
        out[at : at + 16, :] = turned[s * 16 : (s + 1) * 16, :]
        out[at + 16 : at + 24, :] = d_rows
        out[at + 24 : at + 26, :] = gi_turned[s * 2 : (s + 1) * 2, :]
        out[at + 26 : at + 27, :] = w1_row
        out[at + 27 : at + 28, :] = last[s : s + 1, :]


def spread_kernel(
    got, parent, gam, table, out, field_out, d_out, w1_out, own_out, places_out, column_out,
    g_ref, k_ref,
):
    for w in range(8):
        for half in range(2):
            lanes = slice(half * 128, (half + 1) * 128)
            first = [((half * 4 + g) * 8 + w) * 28 for g in range(4)]
            pieces = swapped([got[at : at + 28, :] for at in first])
            for k in range(4):
                piece = pieces[k]
                at = w * 32 + k * 8
                d_out[at : at + 8, lanes] = piece[16:24]
                for h in range(2):
                    field_out[h * 256 + at : h * 256 + at + 8, lanes] = (
                        piece[h * 8 : (h + 1) * 8] * piece[16:24]
                    )
            for h in range(2):
                own_out[w * 2 + h : w * 2 + h + 1, lanes] = pieces[h][27:28]
                own_out[16 + w * 2 + h : 17 + w * 2 + h, lanes] = pieces[2][27:28]
                own_out[32 + w * 2 + h : 33 + w * 2 + h, lanes] = pieces[3][27:28]
    for g in range(8):
        for side in range(2):
            lanes = slice(side * 128, (side + 1) * 128)
            first = [(g * 8 + side * 4 + i) * 28 + 24 for i in range(4)]
            pieces = swapped([got[at : at + 4, :] for at in first])
            for k in range(4):
                for h in range(2):
                    at = h * 32 + g * 4 + k
                    g_ref[at : at + 1, lanes] = pieces[k][h : h + 1] * pieces[k][2:3]
                k_ref[g * 4 + k : g * 4 + k + 1, lanes] = pieces[k][2:3]
    g_ref[64:128, :] = g_ref[0:64, :]
    for i in range(1, 4):
        k_ref[i * 32 : (i + 1) * 32, :] = k_ref[0:32, :]
    w1 = turned_square(k_ref)
    column = jnp.broadcast_to(parent[...].astype(F32), (128, 256)).T
    column_out[...] = column
    same = same_parent(parent[...], column)
    places_out[...] = jnp.broadcast_to(gam[...].astype(F32), (128, 256)).T
    groups = group_flags(parent[...])
    flags = category_flags(gam[...])
    lane = iota((256, 256), 0)
    at = parent[...] // 4 * 32 + parent[...] % 4
    corner = own_out[32:48, :]
    odd = iota((16, 256), 0) % 2 == 1
    y0 = own_out[0:16, :]
    y0 += jnp.where(odd, dot(corner, flag(lane == at + 4)), dot(corner, flag(lane == at)))
    own_out[0:16, :] = y0
    own_out[32:48, :] = dot(corner, flag(lane == at + 8))
    d = d_out[...]
    w1_lifted = ungrouped(w1, groups[0:1])[0]
    w1_out[...] = w1_lifted
    lifted = ungrouped(turned_square(g_ref), groups)
    field = [field_out[h * 256 : (h + 1) * 256, :] + lifted[h] for h in range(2)]
    for h in range(2):
        field_out[h * 256 : (h + 1) * 256, :] = field[h]
    totals = [categories(field, flags)]
    for _ in range(2):
        field = mixed(field, d, w1_lifted, same)
        totals.append(categories(field, flags))
    plain = flag(iota((32, 256), 0) == gam[...])
    everywhere = flag(iota((128, 256), 0) % 32 == parent[...])
    members = lax.dot_general(
        jnp.ones((8, 256), BF16), everywhere, LANES, preferred_element_type=F32
    )[0:1]
    small = [dot(plain, v) for v in (d, d * d, d * w1_lifted)]
    row, lane = iota((128, 256), 0), iota((128, 256), 1)
    at = jnp.where(row < 32, row // 4 * 32 + row % 4, -16)
    small.append(
        dot(dot(plain, w1), flag(lane == at + 8))
        + dot(dot(plain, members * w1 * w1), flag(lane == at + 12))
    )
    count = jnp.sum((table[...] >= 0).astype(F32), axis=1, keepdims=True)
    count = jnp.where(iota((32, 1), 0) % 8 // 2 == lax.axis_index("far"), count, 0.0)
    for w in range(8):
        part = count[w // 2 * 8 : w // 2 * 8 + 8]
        part = jnp.where(iota((8, 1), 0) % 2 == w % 2, part, 0.0)
        size = jnp.sum(part, axis=0, keepdims=True)
        own_out[48 + w * 2 : 50 + w * 2, :] = jnp.broadcast_to(size, (2, 256))
    for z in range(4):
        for i in range(3):
            out[z, i * 16 : (i + 1) * 16, :] = totals[i][z * 16 : (z + 1) * 16]
        out[z, 48:64, :] = y0
        for i in range(4):
            out[z, 64 + i * 8 : 72 + i * 8, :] = small[i][z * 8 : (z + 1) * 8]


def lane_sums(value):
    rows = jnp.sum(value, axis=0, keepdims=True)
    return sum(rows[:, t * 128 : (t + 1) * 128] for t in range(value.shape[1] // 128))


def field_product(a, b):
    return lane_sums(a[0] * b[0] + a[1] * b[1])


def middle_kernel(
    got, field_in, d_in, w1_in, own, places_in, column, parent, out, r0_out, br_out
):
    total = sum(got[z, 0:48, :] for z in range(4))
    small = sum(got[z, 64:96, :] for z in range(4))
    v0, v1, v2 = (total[i * 16 : (i + 1) * 16] for i in range(3))

    def repeated(value):
        return jnp.concatenate(
            [jnp.broadcast_to(value[w : w + 1], (2, 256)) for w in range(8)], axis=0
        )

    y0, w2, w3, n = (own[i * 16 : (i + 1) * 16, :] for i in range(4))
    lane = iota((256, 256), 0)
    at = parent[...] // 4 * 32 + parent[...] % 4
    vd, vd2, e = (repeated(small[i * 8 : (i + 1) * 8]) for i in range(3))
    vw, vw2 = (repeated(dot(small[24:32], flag(lane == at + i))) for i in (8, 12))
    same = same_parent(parent[...], column[...])
    g0 = v0 + n * y0
    shared = dot(jnp.concatenate([y0, e * y0, g0], axis=0), same)
    b1 = v1 + vd * y0 + vw * shared[0:16]
    b2 = v2 + vd2 * y0 + (e + vw2) * shared[0:16] + shared[16:32]
    y1 = w2 * g0 + w3 * shared[32:48]
    g1 = b1 + n * y1
    shared = dot(jnp.concatenate([y1, g1], axis=0), same)
    k1 = vd * y1 + vw * shared[0:16]
    y2 = w2 * g1 + w3 * shared[16:32]
    m1 = lane_sums(g0 * y1)
    m2 = lane_sums((2.0 * b1 + n * y1) * y1)
    m3 = lane_sums((2.0 * b2 + k1) * y1 + g1 * y2)

    d, w1 = d_in[...], w1_in[...]
    shares = jnp.concatenate([got[z, 48:64, :] for z in range(4)], axis=0)
    lifted = lifted_categories(shares, places_in[...])
    field = steps(field_in)
    r0 = [field[h] + lifted[h] for h in range(2)]
    br = mixed(r0, d, w1, same)
    for h in range(2):
        r0_out[h * 256 : (h + 1) * 256, :] = r0[h]
        br_out[h * 256 : (h + 1) * 256, :] = br[h]
    m0 = field_product(r0, r0)
    m1 += field_product(r0, br)
    m2 += field_product(br, br)
    m3 += field_product(br, mixed(br, d, w1, same))
    moments = jnp.concatenate([m0, m1, m2, m3, jnp.zeros((4, 128), F32)], axis=0)
    moments = jnp.sum(moments, axis=1, keepdims=True)
    at_lane = iota((8, 128), 0) == iota((8, 128), 1)
    moments = jnp.sum(jnp.where(at_lane, moments, 0.0), axis=0, keepdims=True)
    for z in range(4):
        at = z * 66
        for t in range(2):
            out[at + t * 16 : at + (t + 1) * 16, :] = y1[:, t * 128 : (t + 1) * 128]
            out[at + 32 + t * 16 : at + 48 + t * 16, :] = y2[:, t * 128 : (t + 1) * 128]
        out[at + 64 : at + 66, :] = jnp.concatenate([moments] * 2, axis=0)


def fields_kernel(got, r0_in, br_in, d_in, w1_in, places_in, column, parent, out):
    same, category = same_parent(parent[...], column[...]), places_in[...]

    def shares(first):
        tiles = [
            jnp.concatenate([got[z * 66 + at : z * 66 + at + 16, :] for z in range(4)], axis=0)
            for at in (first, first + 16)
        ]
        return jnp.concatenate(tiles, axis=1)

    first = lifted_categories(shares(0), category)
    second = lifted_categories(shares(32), category)
    br = steps(br_in)
    field = [br[h] + first[h] for h in range(2)]
    after = mixed(field, d_in[...], w1_in[...], same)
    after = [after[h] + second[h] for h in range(2)]
    moments = sum(got[z * 66 + 64 : z * 66 + 65, :] for z in range(4))
    rows = []
    for one in (steps(r0_in), field, after):
        for half in range(2):
            lanes = slice(half * 128, (half + 1) * 128)
            tiles = [v.reshape(8, 4, 8, 256) for v in one]
            k = [jnp.concatenate([t[:, i] for t in tiles], axis=0) for i in range(4)]
            k = [v.reshape(128, 256)[:, lanes] for v in k]
            rows += [jnp.concatenate(k[0:2], axis=1), jnp.concatenate(k[2:4], axis=1)]
    rows = jnp.concatenate(rows, axis=0)
    source, target = iota((256, 256), 0), iota((256, 256), 1)
    group = source // 32
    place = (group & 1) * 128 + ((group & 2) | (group // 4)) * 32 + source % 32
    moves = flag(target == place)
    high = rows.astype(BF16)
    rest = rows - high.astype(F32)
    rows = jnp.dot(
        jnp.concatenate([high, *parts(rest)], axis=1),
        jnp.concatenate([moves] * 3, axis=0),
        preferred_element_type=F32,
    )
    upper = iota((128, 128), 1) >= 64
    for i in range(3):
        for half in range(2):
            at = (i * 2 + half) * 256
            pieces = [None] * 4
            for j in range(2):
                a, b = (rows[at + p : at + p + 128, j * 128 : (j + 1) * 128] for p in (0, 128))
                moved = pltpu.roll(jnp.where(upper, a, b), 64, 1)
                pieces[j] = jnp.where(upper, moved, a)
                pieces[j + 2] = jnp.where(upper, b, moved)
            for g in range(4):
                for w in range(8):
                    to = ((half * 4 + g) * 8 + w) * 49 + i * 16
                    for h in range(2):
                        out[to + h * 8 : to + h * 8 + 8, :] = pieces[g][
                            (h * 8 + w) * 8 : (h * 8 + w) * 8 + 8
                        ]
    for s in range(64):
        out[s * 49 + 48 : s * 49 + 49, :] = moments


def finish_kernel(got, x_out, r_out, x_ref, r_ref, turned, sems):
    sums = [
        sum(got[s * 49 + 48 : s * 49 + 49, :] for s in range(i, 64, 8)) for i in range(8)
    ]
    m = sum(sums)
    m0, m1, m2, m3 = (m[:, i : i + 1] for i in range(4))
    alpha = m0 / m1
    norm = m0 - 2.0 * alpha * m1 + alpha * alpha * m2
    grown = 1.0 + norm / m0
    product = grown * grown * m1 - 2.0 * grown * alpha * m2 + alpha * alpha * m3
    later = norm / product
    on_first, on_second = alpha + later * grown, -later * alpha
    for s in range(64):
        first, second, third = (got[s * 49 + i * 16 : s * 49 + i * 16 + 16, :] for i in range(3))
        x_ref[s * 16 : (s + 1) * 16, :] = on_first * first + on_second * second
        r_ref[s * 16 : (s + 1) * 16, :] = first - on_first * second - on_second * third
    copies = []
    for j, (ref, out) in enumerate(((x_ref, x_out), (r_ref, r_out))):
        for i in range(8):
            block = ref[pl.ds(i, 128, stride=8), :].T
            for k in range(4):
                turned[pl.ds(j * 1024 + k * 8 + i, 32, stride=32), :] = block[
                    k * 32 : (k + 1) * 32
                ]
        copy = pltpu.make_async_copy(turned.at[pl.ds(j * 1024, 1024), :], out, sems.at[j])
        copy.start()
        copies.append(copy)
    for copy in copies:
        copy.wait()


def call(kernel, outs, scratch=(), kept=(), last=False):
    vmem = pl.BlockSpec(memory_space=pltpu.VMEM)
    kind = jax.ShapeDtypeStruct if last else pltpu.VMEM

    def run(*args):
        args = [
            pltpu.with_memory_space_constraint(a, pltpu.VMEM) if i in kept else a
            for i, a in enumerate(args)
        ]
        return pl.pallas_call(
            kernel,
            out_shape=tuple(kind(shape, F32) for shape in outs),
            in_specs=[vmem] * len(args),
            out_specs=(pl.BlockSpec(memory_space=pl.ANY) if last else vmem,) * len(outs),
            scratch_shapes=[pltpu.VMEM(shape, F32) for shape in scratch]
            + [pltpu.SemaphoreType.DMA((2,))] * last,
            compiler_params=pltpu.CompilerParams(vmem_limit_bytes=(16 if kept else 58) << 20),
        )(*args)

    return run


def exchanged(value, axes, blocks, tile):
    shape = value.shape
    value = value.reshape(blocks, -1, tile, shape[-1])
    return lax.all_to_all(value, axes, 0, 0, tiled=True).reshape(shape)


def row_of(table, wanted, names):
    hit = table[:, :, None] == wanted[None, None, :]
    return jnp.sum(jnp.where(hit, names[:, None, None], 0), axis=(0, 1), dtype=jnp.int32)[None]


def on_device(b, gi, ac, gc, d, w1, w2, w3, group_table, class_table):
    (sent,) = call(pack_kernel, [(64 * 28, 128)], [(1024, 128), (128, 128)])(
        b.reshape(1024, 128),
        d,
        gi.reshape(128, 128),
        w1,
        ac.reshape(32, 128),
        w2.reshape(1, 32),
        gc,
        w3,
    )
    got = exchanged(sent, SPLIT, 64, 4)
    category = jnp.arange(32, dtype=jnp.int32)
    lane = jnp.arange(256, dtype=jnp.int32)
    parent = row_of(group_table, lane, category)
    product = lane // 64 * 256 + lax.axis_index("far") * 64 + lane % 64
    place = category % 8 // 2 * 8 + category // 8 * 2 + category % 2
    gam = row_of(class_table, product, place)
    sent, field, d_all, w1_all, own, places, column = call(
        spread_kernel,
        [(4, 96, 256), (512, 256), (256, 256), (256, 256), (64, 256), (256, 128), (256, 128)],
        [(128, 256), (128, 256)],
        kept=(0,),
    )(got, parent, gam, class_table)
    got = exchanged(sent, "far", 4, 8)
    sent, r0, br = call(middle_kernel, [(4 * 66, 128), (512, 256), (512, 256)], kept=range(7))(
        got, field, d_all, w1_all, own, places, column, parent
    )
    got = exchanged(sent, "far", 4, 2)
    (sent,) = call(fields_kernel, [(64 * 49, 128)], kept=range(7))(
        got, r0, br, d_all, w1_all, places, column, parent
    )
    got = exchanged(sent, SPLIT, 64, 1)
    solution_field, residual = call(
        finish_kernel,
        [(1024, 128)] * 2,
        [(1024, 128), (1024, 128), (2048, 128)],
        kept=(0,),
        last=True,
    )(got)
    return solution_field.reshape(32, 32, 128), residual.reshape(32, 32, 128)


def solution(mesh):
    finer = Mesh(
        mesh.devices.reshape(4, 2, 4, 4, 2), ("y", "core", "x", "far", "near")
    )
    return jax.shard_map(
        on_device,
        mesh=finer,
        in_specs=(
            P(REG, PROD, None),
            P(REG, PROD, None),
            P(REG, PROD, None),
            P(REG, None, None),
            P(REG, PROD),
            P(REG, PROD),
            P(REG, PROD),
            P(REG, None),
            P(),
            P(),
        ),
        out_specs=(P(REG, PROD, None), P(REG, PROD, None)),
        check_vma=False,
    )
```

```python
import jax
import jax.numpy as jnp
from jax import lax
from jax.experimental import pallas as pl
from jax.experimental.pallas import tpu as pltpu
from jax.sharding import Mesh
from jax.sharding import PartitionSpec as P

F32 = jnp.float32
BF16 = jnp.bfloat16
REG = ("y", "core")
PROD = ("x", "far", "near")
SPLIT = ("core", "y", "x", "near")
LANES = (((1,), (1,)), ((), ()))


def sender(block, w):
    return block % 2 * 32 + block // 2 * 8 + w


def iota(shape, dim):
    return lax.broadcasted_iota(jnp.int32, shape, dim)


def flag(condition):
    return condition.astype(F32).astype(BF16)


def parts(value):
    high = value.astype(BF16)
    return high, (value - high.astype(F32)).astype(BF16)


def dot(a, b):
    if a.dtype == BF16:
        a, b = jnp.concatenate([a, a], axis=1), jnp.concatenate(parts(b), axis=0)
    else:
        a, b = jnp.concatenate(parts(a), axis=1), jnp.concatenate([b, b], axis=0)
    return jnp.dot(a, b, preferred_element_type=F32)


def swapped(pieces):
    group = iota(pieces[0].shape, 1) // 32
    odd, upper = (group & 1) == 1, group >= 2
    a = []
    for i in (0, 2):
        a.append(jnp.where(odd, pltpu.roll(pieces[i + 1], 32, 1), pieces[i]))
        a.append(jnp.where(odd, pieces[i + 1], pltpu.roll(pieces[i], 96, 1)))
    low, high = [], []
    for i in range(2):
        moved = pltpu.roll(jnp.where(upper, a[i], a[i + 2]), 64, 1)
        low.append(jnp.where(upper, moved, a[i]))
        high.append(jnp.where(upper, a[i + 2], moved))
    return low + high


def group_flags(parent):
    row = iota((128, 256), 0) % 64
    return [flag(row == parent + 32 * h) for h in range(2)]


def category_flags(places):
    row = iota((64, 256), 0)
    return [flag(row == places * 2 + h) for h in range(2)]


def ungrouped(value, flags):
    high = value.astype(BF16).astype(F32)
    both = jnp.where(iota(value.shape, 1) < 64, high, value - high).astype(BF16)
    return [jnp.dot(both, f, preferred_element_type=F32) for f in flags]


def same_parent(parent, column):
    column = jnp.concatenate([column, column], axis=1)
    return flag(column == parent.astype(F32))


def mixed(field, precision, group_precision, same):
    return [precision * v + group_precision * dot(v, same) for v in field]


def categories(field, flags):
    return dot(flags[0], field[0]) + dot(flags[1], field[1])


def lifted_categories(value, places):
    both = jnp.concatenate(parts(value), axis=0)
    lane = (iota((256, 128), 1) % 64).astype(F32)
    flags = [flag(lane == places * 2.0 + h) for h in range(2)]
    return [jnp.dot(f, both, preferred_element_type=F32) for f in flags]


def steps(ref):
    return [ref[h * 256 : (h + 1) * 256, :] for h in range(2)]


def turned_square(ref):
    return jnp.concatenate([ref[:, 0:128].T, ref[:, 128:256].T], axis=0)


def pack_kernel(b, d, gi, w1, ac, w2, gc, w3, out, turned, turned_small):
    own = lax.axis_index("x") * 8 + lax.axis_index("far") * 2 + lax.axis_index("near")
    for i in range(8):
        block = jnp.concatenate(
            [b[pl.ds(k * 8 + i, 32, stride=32), :] for k in range(4)], axis=0
        )
        turned[pl.ds(i, 128, stride=8), :] = block.T
    d_turned = d[...].T
    d_rows = jnp.concatenate([d_turned[k * 8 : (k + 1) * 8] for k in range(4)], axis=1)
    w1_row = jnp.concatenate([w1[k : k + 1, :] for k in range(4)], axis=1)
    w2_row = jnp.concatenate([w2[...]] * 4, axis=1)
    gi_turned = gi[...].T
    mine = (iota((4, 32, 128), 1) == own).astype(F32)
    corner = jnp.sum(gc[...] * mine, axis=1)
    weight = jnp.sum(jnp.where(iota((4, 32), 1) == own, w3[...], 0.0), axis=1, keepdims=True)
    small = [ac[...], corner * weight, jnp.broadcast_to(weight, (4, 128))]
    small = jnp.concatenate([*small, jnp.zeros((88, 128), F32)], axis=0)
    turned_small[...] = small.T
    first, second = (turned_small[pl.ds(h, 64, stride=2), :] for h in range(2))
    corners = jnp.concatenate(
        [first[:, 32:36], second[:, 32:36], first[:, 36:40], jnp.zeros((64, 20), F32)], axis=1
    )
    last = jnp.concatenate([first[:, 0:32], second[:, 0:32], first[:, 0:32], corners], axis=1)
    lane = iota((64, 128), 1)
    last = jnp.where(lane < 96, jnp.where(lane < 64, last * w2_row, w2_row), last)
    for s in range(64):
        at = s * 28
        out[at : at + 16, :] = turned[s * 16 : (s + 1) * 16, :]
        out[at + 16 : at + 24, :] = d_rows
        out[at + 24 : at + 26, :] = gi_turned[s * 2 : (s + 1) * 2, :]
        out[at + 26 : at + 27, :] = w1_row
        out[at + 27 : at + 28, :] = last[s : s + 1, :]


def spread_kernel(
    got, parent, gam, table, out, field_out, d_out, w1_out, own_out, places_out, column_out,
    g_ref, k_ref,
):
    for w in range(8):
        for half in range(2):
            lanes = slice(half * 128, (half + 1) * 128)
            first = [sender(half * 4 + g, w) * 28 for g in range(4)]
            pieces = swapped([got[at : at + 28, :] for at in first])
            for k in range(4):
                piece = pieces[k]
                at = w * 32 + k * 8
                d_out[at : at + 8, lanes] = piece[16:24]
                for h in range(2):
                    field_out[h * 256 + at : h * 256 + at + 8, lanes] = (
                        piece[h * 8 : (h + 1) * 8] * piece[16:24]
                    )
            for h in range(2):
                own_out[w * 2 + h : w * 2 + h + 1, lanes] = pieces[h][27:28]
                own_out[16 + w * 2 + h : 17 + w * 2 + h, lanes] = pieces[2][27:28]
                own_out[32 + w * 2 + h : 33 + w * 2 + h, lanes] = pieces[3][27:28]
    for g in range(8):
        for side in range(2):
            lanes = slice(side * 128, (side + 1) * 128)
            first = [sender(g, side * 4 + i) * 28 + 24 for i in range(4)]
            pieces = swapped([got[at : at + 4, :] for at in first])
            for k in range(4):
                for h in range(2):
                    at = h * 32 + g * 4 + k
                    g_ref[at : at + 1, lanes] = pieces[k][h : h + 1] * pieces[k][2:3]
                k_ref[g * 4 + k : g * 4 + k + 1, lanes] = pieces[k][2:3]
    g_ref[64:128, :] = g_ref[0:64, :]
    for i in range(1, 4):
        k_ref[i * 32 : (i + 1) * 32, :] = k_ref[0:32, :]
    w1 = turned_square(k_ref)
    column = jnp.broadcast_to(parent[...].astype(F32), (128, 256)).T
    column_out[...] = column
    same = same_parent(parent[...], column)
    places_out[...] = jnp.broadcast_to(gam[...].astype(F32), (128, 256)).T
    groups = group_flags(parent[...])
    flags = category_flags(gam[...])
    lane = iota((256, 256), 0)
    at = parent[...] // 4 * 32 + parent[...] % 4
    corner = own_out[32:48, :]
    odd = iota((16, 256), 0) % 2 == 1
    y0 = own_out[0:16, :]
    y0 += jnp.where(odd, dot(corner, flag(lane == at + 4)), dot(corner, flag(lane == at)))
    own_out[0:16, :] = y0
    own_out[32:48, :] = dot(corner, flag(lane == at + 8))
    d = d_out[...]
    w1_lifted = ungrouped(w1, groups[0:1])[0]
    w1_out[...] = w1_lifted
    lifted = ungrouped(turned_square(g_ref), groups)
    field = [field_out[h * 256 : (h + 1) * 256, :] + lifted[h] for h in range(2)]
    for h in range(2):
        field_out[h * 256 : (h + 1) * 256, :] = field[h]
    totals = [categories(field, flags)]
    for _ in range(2):
        field = mixed(field, d, w1_lifted, same)
        totals.append(categories(field, flags))
    plain = flag(iota((32, 256), 0) == gam[...])
    everywhere = flag(iota((128, 256), 0) % 32 == parent[...])
    members = lax.dot_general(
        jnp.ones((8, 256), BF16), everywhere, LANES, preferred_element_type=F32
    )[0:1]
    small = [dot(plain, v) for v in (d, d * d, d * w1_lifted)]
    row, lane = iota((128, 256), 0), iota((128, 256), 1)
    at = jnp.where(row < 32, row // 4 * 32 + row % 4, -16)
    small.append(
        dot(dot(plain, w1), flag(lane == at + 8))
        + dot(dot(plain, members * w1 * w1), flag(lane == at + 12))
    )
    count = jnp.sum((table[...] >= 0).astype(F32), axis=1, keepdims=True)
    count = jnp.where(iota((32, 1), 0) % 8 // 2 == lax.axis_index("far"), count, 0.0)
    for w in range(8):
        part = count[w // 2 * 8 : w // 2 * 8 + 8]
        part = jnp.where(iota((8, 1), 0) % 2 == w % 2, part, 0.0)
        size = jnp.sum(part, axis=0, keepdims=True)
        own_out[48 + w * 2 : 50 + w * 2, :] = jnp.broadcast_to(size, (2, 256))
    for z in range(4):
        for i in range(3):
            out[z, i * 16 : (i + 1) * 16, :] = totals[i][z * 16 : (z + 1) * 16]
        out[z, 48:64, :] = y0
        for i in range(4):
            out[z, 64 + i * 8 : 72 + i * 8, :] = small[i][z * 8 : (z + 1) * 8]


def lane_sums(value):
    rows = jnp.sum(value, axis=0, keepdims=True)
    return sum(rows[:, t * 128 : (t + 1) * 128] for t in range(value.shape[1] // 128))


def field_product(a, b):
    return lane_sums(a[0] * b[0] + a[1] * b[1])


def middle_kernel(
    got, field_in, d_in, w1_in, own, places_in, column, parent, out, r0_out, br_out
):
    total = sum(got[z, 0:48, :] for z in range(4))
    small = sum(got[z, 64:96, :] for z in range(4))
    v0, v1, v2 = (total[i * 16 : (i + 1) * 16] for i in range(3))

    def repeated(value):
        return jnp.concatenate(
            [jnp.broadcast_to(value[w : w + 1], (2, 256)) for w in range(8)], axis=0
        )

    y0, w2, w3, n = (own[i * 16 : (i + 1) * 16, :] for i in range(4))
    lane = iota((256, 256), 0)
    at = parent[...] // 4 * 32 + parent[...] % 4
    vd, vd2, e = (repeated(small[i * 8 : (i + 1) * 8]) for i in range(3))
    vw, vw2 = (repeated(dot(small[24:32], flag(lane == at + i))) for i in (8, 12))
    same = same_parent(parent[...], column[...])
    g0 = v0 + n * y0
    shared = dot(jnp.concatenate([y0, e * y0, g0], axis=0), same)
    b1 = v1 + vd * y0 + vw * shared[0:16]
    b2 = v2 + vd2 * y0 + (e + vw2) * shared[0:16] + shared[16:32]
    y1 = w2 * g0 + w3 * shared[32:48]
    g1 = b1 + n * y1
    shared = dot(jnp.concatenate([y1, g1], axis=0), same)
    k1 = vd * y1 + vw * shared[0:16]
    y2 = w2 * g1 + w3 * shared[16:32]
    m1 = lane_sums(g0 * y1)
    m2 = lane_sums((2.0 * b1 + n * y1) * y1)
    m3 = lane_sums((2.0 * b2 + k1) * y1 + g1 * y2)

    d, w1 = d_in[...], w1_in[...]
    shares = jnp.concatenate([got[z, 48:64, :] for z in range(4)], axis=0)
    lifted = lifted_categories(shares, places_in[...])
    field = steps(field_in)
    r0 = [field[h] + lifted[h] for h in range(2)]
    br = mixed(r0, d, w1, same)
    for h in range(2):
        r0_out[h * 256 : (h + 1) * 256, :] = r0[h]
        br_out[h * 256 : (h + 1) * 256, :] = br[h]
    m0 = field_product(r0, r0)
    m1 += field_product(r0, br)
    m2 += field_product(br, br)
    m3 += field_product(br, mixed(br, d, w1, same))
    moments = jnp.concatenate([m0, m1, m2, m3, jnp.zeros((4, 128), F32)], axis=0)
    moments = jnp.sum(moments, axis=1, keepdims=True)
    at_lane = iota((8, 128), 0) == iota((8, 128), 1)
    moments = jnp.sum(jnp.where(at_lane, moments, 0.0), axis=0, keepdims=True)
    for z in range(4):
        at = z * 66
        for t in range(2):
            out[at + t * 16 : at + (t + 1) * 16, :] = y1[:, t * 128 : (t + 1) * 128]
            out[at + 32 + t * 16 : at + 48 + t * 16, :] = y2[:, t * 128 : (t + 1) * 128]
        out[at + 64 : at + 66, :] = jnp.concatenate([moments] * 2, axis=0)


def fields_kernel(got, r0_in, br_in, d_in, w1_in, places_in, column, parent, out):
    same, category = same_parent(parent[...], column[...]), places_in[...]

    def shares(first):
        tiles = [
            jnp.concatenate([got[z * 66 + at : z * 66 + at + 16, :] for z in range(4)], axis=0)
            for at in (first, first + 16)
        ]
        return jnp.concatenate(tiles, axis=1)

    first = lifted_categories(shares(0), category)
    second = lifted_categories(shares(32), category)
    br = steps(br_in)
    field = [br[h] + first[h] for h in range(2)]
    after = mixed(field, d_in[...], w1_in[...], same)
    after = [after[h] + second[h] for h in range(2)]
    moments = sum(got[z * 66 + 64 : z * 66 + 65, :] for z in range(4))
    rows = []
    for one in (steps(r0_in), field, after):
        for half in range(2):
            lanes = slice(half * 128, (half + 1) * 128)
            tiles = [v.reshape(8, 4, 8, 256) for v in one]
            k = [jnp.concatenate([t[:, i] for t in tiles], axis=0) for i in range(4)]
            k = [v.reshape(128, 256)[:, lanes] for v in k]
            rows += [jnp.concatenate(k[0:2], axis=1), jnp.concatenate(k[2:4], axis=1)]
    rows = jnp.concatenate(rows, axis=0)
    source, target = iota((256, 256), 0), iota((256, 256), 1)
    group = source // 32
    place = (group & 1) * 128 + ((group & 2) | (group // 4)) * 32 + source % 32
    moves = flag(target == place)
    high = rows.astype(BF16)
    rest = rows - high.astype(F32)
    rows = jnp.dot(
        jnp.concatenate([high, *parts(rest)], axis=1),
        jnp.concatenate([moves] * 3, axis=0),
        preferred_element_type=F32,
    )
    upper = iota((128, 128), 1) >= 64
    for i in range(3):
        for half in range(2):
            at = (i * 2 + half) * 256
            pieces = [None] * 4
            for j in range(2):
                a, b = (rows[at + p : at + p + 128, j * 128 : (j + 1) * 128] for p in (0, 128))
                moved = pltpu.roll(jnp.where(upper, a, b), 64, 1)
                pieces[j] = jnp.where(upper, moved, a)
                pieces[j + 2] = jnp.where(upper, b, moved)
            for g in range(4):
                for w in range(8):
                    to = sender(half * 4 + g, w) * 49 + i * 16
                    for h in range(2):
                        out[to + h * 8 : to + h * 8 + 8, :] = pieces[g][
                            (h * 8 + w) * 8 : (h * 8 + w) * 8 + 8
                        ]
    for s in range(64):
        out[s * 49 + 48 : s * 49 + 49, :] = moments


def finish_kernel(got, x_out, r_out, x_ref, r_ref, turned, sems):
    sums = [
        sum(got[s * 49 + 48 : s * 49 + 49, :] for s in range(i, 64, 8)) for i in range(8)
    ]
    m = sum(sums)
    m0, m1, m2, m3 = (m[:, i : i + 1] for i in range(4))
    alpha = m0 / m1
    norm = m0 - 2.0 * alpha * m1 + alpha * alpha * m2
    grown = 1.0 + norm / m0
    product = grown * grown * m1 - 2.0 * grown * alpha * m2 + alpha * alpha * m3
    later = norm / product
    on_first, on_second = alpha + later * grown, -later * alpha
    for s in range(64):
        first, second, third = (got[s * 49 + i * 16 : s * 49 + i * 16 + 16, :] for i in range(3))
        x_ref[s * 16 : (s + 1) * 16, :] = on_first * first + on_second * second
        r_ref[s * 16 : (s + 1) * 16, :] = first - on_first * second - on_second * third
    copies = []
    for j, (ref, out) in enumerate(((x_ref, x_out), (r_ref, r_out))):
        for i in range(8):
            block = ref[pl.ds(i, 128, stride=8), :].T
            for k in range(4):
                turned[pl.ds(j * 1024 + k * 8 + i, 32, stride=32), :] = block[
                    k * 32 : (k + 1) * 32
                ]
        copy = pltpu.make_async_copy(turned.at[pl.ds(j * 1024, 1024), :], out, sems.at[j])
        copy.start()
        copies.append(copy)
    for copy in copies:
        copy.wait()


def call(kernel, outs, scratch=(), kept=(), last=False):
    vmem = pl.BlockSpec(memory_space=pltpu.VMEM)
    kind = jax.ShapeDtypeStruct if last else pltpu.VMEM

    def run(*args):
        args = [
            pltpu.with_memory_space_constraint(a, pltpu.VMEM) if i in kept else a
            for i, a in enumerate(args)
        ]
        return pl.pallas_call(
            kernel,
            out_shape=tuple(kind(shape, F32) for shape in outs),
            in_specs=[vmem] * len(args),
            out_specs=(pl.BlockSpec(memory_space=pl.ANY) if last else vmem,) * len(outs),
            scratch_shapes=[pltpu.VMEM(shape, F32) for shape in scratch]
            + [pltpu.SemaphoreType.DMA((2,))] * last,
            compiler_params=pltpu.CompilerParams(vmem_limit_bytes=(16 if kept else 58) << 20),
        )(*args)

    return run


def exchanged(value, axes, blocks, tile):
    shape = value.shape
    value = value.reshape(blocks, -1, tile, shape[-1])
    return lax.all_to_all(value, axes, 0, 0, tiled=True).reshape(shape)


def row_of(table, wanted, names):
    hit = table[:, :, None] == wanted[None, None, :]
    return jnp.sum(jnp.where(hit, names[:, None, None], 0), axis=(0, 1), dtype=jnp.int32)[None]


def on_device(b, gi, ac, gc, d, w1, w2, w3, group_table, class_table):
    (sent,) = call(pack_kernel, [(64 * 28, 128)], [(1024, 128), (128, 128)])(
        b.reshape(1024, 128),
        d,
        gi.reshape(128, 128),
        w1,
        ac.reshape(32, 128),
        w2.reshape(1, 32),
        gc,
        w3,
    )
    got = exchanged(sent, SPLIT, 64, 4)
    category = jnp.arange(32, dtype=jnp.int32)
    lane = jnp.arange(256, dtype=jnp.int32)
    parent = row_of(group_table, lane, category)
    product = lane // 64 * 256 + lax.axis_index("far") * 64 + lane % 64
    place = category % 8 // 2 * 8 + category // 8 * 2 + category % 2
    gam = row_of(class_table, product, place)
    sent, field, d_all, w1_all, own, places, column = call(
        spread_kernel,
        [(4, 96, 256), (512, 256), (256, 256), (256, 256), (64, 256), (256, 128), (256, 128)],
        [(128, 256), (128, 256)],
        kept=(0,),
    )(got, parent, gam, class_table)
    got = exchanged(sent, "far", 4, 8)
    sent, r0, br = call(middle_kernel, [(4 * 66, 128), (512, 256), (512, 256)], kept=range(7))(
        got, field, d_all, w1_all, own, places, column, parent
    )
    got = exchanged(sent, "far", 4, 2)
    (sent,) = call(fields_kernel, [(64 * 49, 128)], kept=range(7))(
        got, r0, br, d_all, w1_all, places, column, parent
    )
    got = exchanged(sent, SPLIT, 64, 1)
    solution_field, residual = call(
        finish_kernel,
        [(1024, 128)] * 2,
        [(1024, 128), (1024, 128), (2048, 128)],
        kept=(0,),
        last=True,
    )(got)
    return solution_field.reshape(32, 32, 128), residual.reshape(32, 32, 128)


def solution(mesh):
    finer = Mesh(
        mesh.devices.reshape(4, 2, 4, 4, 2), ("y", "core", "x", "far", "near")
    )
    return jax.shard_map(
        on_device,
        mesh=finer,
        in_specs=(
            P(REG, PROD, None),
            P(REG, PROD, None),
            P(REG, PROD, None),
            P(REG, None, None),
            P(REG, PROD),
            P(REG, PROD),
            P(REG, PROD),
            P(REG, None),
            P(),
            P(),
        ),
        out_specs=(P(REG, PROD, None), P(REG, PROD, None)),
        check_vma=False,
    )
```

```python
import jax
import jax.numpy as jnp
from jax import lax
from jax.experimental import pallas as pl
from jax.experimental.pallas import tpu as pltpu
from jax.sharding import Mesh
from jax.sharding import PartitionSpec as P

F32 = jnp.float32
BF16 = jnp.bfloat16
REG = ("y", "core")
PROD = ("x", "far", "near")
SPLIT = ("core", "x", "near", "y")
LANES = (((1,), (1,)), ((), ()))


def sender(block, w):
    return block % 2 * 32 + w * 4 + block // 2


def iota(shape, dim):
    return lax.broadcasted_iota(jnp.int32, shape, dim)


def flag(condition):
    return condition.astype(F32).astype(BF16)


def parts(value):
    high = value.astype(BF16)
    return high, (value - high.astype(F32)).astype(BF16)


def dot(a, b):
    if a.dtype == BF16:
        a, b = jnp.concatenate([a, a], axis=1), jnp.concatenate(parts(b), axis=0)
    else:
        a, b = jnp.concatenate(parts(a), axis=1), jnp.concatenate([b, b], axis=0)
    return jnp.dot(a, b, preferred_element_type=F32)


def swapped(pieces):
    group = iota(pieces[0].shape, 1) // 32
    odd, upper = (group & 1) == 1, group >= 2
    a = []
    for i in (0, 2):
        a.append(jnp.where(odd, pltpu.roll(pieces[i + 1], 32, 1), pieces[i]))
        a.append(jnp.where(odd, pieces[i + 1], pltpu.roll(pieces[i], 96, 1)))
    low, high = [], []
    for i in range(2):
        moved = pltpu.roll(jnp.where(upper, a[i], a[i + 2]), 64, 1)
        low.append(jnp.where(upper, moved, a[i]))
        high.append(jnp.where(upper, a[i + 2], moved))
    return low + high


def group_flags(parent):
    row = iota((128, 256), 0) % 64
    return [flag(row == parent + 32 * h) for h in range(2)]


def category_flags(places):
    row = iota((64, 256), 0)
    return [flag(row == places * 2 + h) for h in range(2)]


def ungrouped(value, flags):
    high = value.astype(BF16).astype(F32)
    both = jnp.where(iota(value.shape, 1) < 64, high, value - high).astype(BF16)
    return [jnp.dot(both, f, preferred_element_type=F32) for f in flags]


def same_parent(parent, column):
    column = jnp.concatenate([column, column], axis=1)
    return flag(column == parent.astype(F32))


def mixed(field, precision, group_precision, same):
    return [precision * v + group_precision * dot(v, same) for v in field]


def categories(field, flags):
    return dot(flags[0], field[0]) + dot(flags[1], field[1])


def lifted_categories(value, places):
    both = jnp.concatenate(parts(value), axis=0)
    lane = (iota((256, 128), 1) % 64).astype(F32)
    flags = [flag(lane == places * 2.0 + h) for h in range(2)]
    return [jnp.dot(f, both, preferred_element_type=F32) for f in flags]


def steps(ref):
    return [ref[h * 256 : (h + 1) * 256, :] for h in range(2)]


def turned_square(ref):
    return jnp.concatenate([ref[:, 0:128].T, ref[:, 128:256].T], axis=0)


def pack_kernel(b, d, gi, w1, ac, w2, gc, w3, out, turned, turned_small):
    own = lax.axis_index("x") * 8 + lax.axis_index("far") * 2 + lax.axis_index("near")
    for i in range(8):
        block = jnp.concatenate(
            [b[pl.ds(k * 8 + i, 32, stride=32), :] for k in range(4)], axis=0
        )
        turned[pl.ds(i, 128, stride=8), :] = block.T
    d_turned = d[...].T
    d_rows = jnp.concatenate([d_turned[k * 8 : (k + 1) * 8] for k in range(4)], axis=1)
    w1_row = jnp.concatenate([w1[k : k + 1, :] for k in range(4)], axis=1)
    w2_row = jnp.concatenate([w2[...]] * 4, axis=1)
    gi_turned = gi[...].T
    mine = (iota((4, 32, 128), 1) == own).astype(F32)
    corner = jnp.sum(gc[...] * mine, axis=1)
    weight = jnp.sum(jnp.where(iota((4, 32), 1) == own, w3[...], 0.0), axis=1, keepdims=True)
    small = [ac[...], corner * weight, jnp.broadcast_to(weight, (4, 128))]
    small = jnp.concatenate([*small, jnp.zeros((88, 128), F32)], axis=0)
    turned_small[...] = small.T
    first, second = (turned_small[pl.ds(h, 64, stride=2), :] for h in range(2))
    corners = jnp.concatenate(
        [first[:, 32:36], second[:, 32:36], first[:, 36:40], jnp.zeros((64, 20), F32)], axis=1
    )
    last = jnp.concatenate([first[:, 0:32], second[:, 0:32], first[:, 0:32], corners], axis=1)
    lane = iota((64, 128), 1)
    last = jnp.where(lane < 96, jnp.where(lane < 64, last * w2_row, w2_row), last)
    for s in range(64):
        at = s * 28
        out[at : at + 16, :] = turned[s * 16 : (s + 1) * 16, :]
        out[at + 16 : at + 24, :] = d_rows
        out[at + 24 : at + 26, :] = gi_turned[s * 2 : (s + 1) * 2, :]
        out[at + 26 : at + 27, :] = w1_row
        out[at + 27 : at + 28, :] = last[s : s + 1, :]


def spread_kernel(
    got, parent, gam, table, out, field_out, d_out, w1_out, own_out, places_out, column_out,
    g_ref, k_ref,
):
    for w in range(8):
        for half in range(2):
            lanes = slice(half * 128, (half + 1) * 128)
            first = [sender(half * 4 + g, w) * 28 for g in range(4)]
            pieces = swapped([got[at : at + 28, :] for at in first])
            for k in range(4):
                piece = pieces[k]
                at = w * 32 + k * 8
                d_out[at : at + 8, lanes] = piece[16:24]
                for h in range(2):
                    field_out[h * 256 + at : h * 256 + at + 8, lanes] = (
                        piece[h * 8 : (h + 1) * 8] * piece[16:24]
                    )
            for h in range(2):
                own_out[w * 2 + h : w * 2 + h + 1, lanes] = pieces[h][27:28]
                own_out[16 + w * 2 + h : 17 + w * 2 + h, lanes] = pieces[2][27:28]
                own_out[32 + w * 2 + h : 33 + w * 2 + h, lanes] = pieces[3][27:28]
    for g in range(8):
        for side in range(2):
            lanes = slice(side * 128, (side + 1) * 128)
            first = [sender(g, side * 4 + i) * 28 + 24 for i in range(4)]
            pieces = swapped([got[at : at + 4, :] for at in first])
            for k in range(4):
                for h in range(2):
                    at = h * 32 + g * 4 + k
                    g_ref[at : at + 1, lanes] = pieces[k][h : h + 1] * pieces[k][2:3]
                k_ref[g * 4 + k : g * 4 + k + 1, lanes] = pieces[k][2:3]
    g_ref[64:128, :] = g_ref[0:64, :]
    for i in range(1, 4):
        k_ref[i * 32 : (i + 1) * 32, :] = k_ref[0:32, :]
    w1 = turned_square(k_ref)
    column = jnp.broadcast_to(parent[...].astype(F32), (128, 256)).T
    column_out[...] = column
    same = same_parent(parent[...], column)
    places_out[...] = jnp.broadcast_to(gam[...].astype(F32), (128, 256)).T
    groups = group_flags(parent[...])
    flags = category_flags(gam[...])
    lane = iota((256, 256), 0)
    at = parent[...] // 4 * 32 + parent[...] % 4
    corner = own_out[32:48, :]
    odd = iota((16, 256), 0) % 2 == 1
    y0 = own_out[0:16, :]
    y0 += jnp.where(odd, dot(corner, flag(lane == at + 4)), dot(corner, flag(lane == at)))
    own_out[0:16, :] = y0
    own_out[32:48, :] = dot(corner, flag(lane == at + 8))
    d = d_out[...]
    w1_lifted = ungrouped(w1, groups[0:1])[0]
    w1_out[...] = w1_lifted
    lifted = ungrouped(turned_square(g_ref), groups)
    field = [field_out[h * 256 : (h + 1) * 256, :] + lifted[h] for h in range(2)]
    for h in range(2):
        field_out[h * 256 : (h + 1) * 256, :] = field[h]
    totals = [categories(field, flags)]
    for _ in range(2):
        field = mixed(field, d, w1_lifted, same)
        totals.append(categories(field, flags))
    plain = flag(iota((32, 256), 0) == gam[...])
    everywhere = flag(iota((128, 256), 0) % 32 == parent[...])
    members = lax.dot_general(
        jnp.ones((8, 256), BF16), everywhere, LANES, preferred_element_type=F32
    )[0:1]
    small = [dot(plain, v) for v in (d, d * d, d * w1_lifted)]
    row, lane = iota((128, 256), 0), iota((128, 256), 1)
    at = jnp.where(row < 32, row // 4 * 32 + row % 4, -16)
    small.append(
        dot(dot(plain, w1), flag(lane == at + 8))
        + dot(dot(plain, members * w1 * w1), flag(lane == at + 12))
    )
    count = jnp.sum((table[...] >= 0).astype(F32), axis=1, keepdims=True)
    count = jnp.where(iota((32, 1), 0) % 8 // 2 == lax.axis_index("far"), count, 0.0)
    for w in range(8):
        part = count[w // 2 * 8 : w // 2 * 8 + 8]
        part = jnp.where(iota((8, 1), 0) % 2 == w % 2, part, 0.0)
        size = jnp.sum(part, axis=0, keepdims=True)
        own_out[48 + w * 2 : 50 + w * 2, :] = jnp.broadcast_to(size, (2, 256))
    for z in range(4):
        for i in range(3):
            out[z, i * 16 : (i + 1) * 16, :] = totals[i][z * 16 : (z + 1) * 16]
        out[z, 48:64, :] = y0
        for i in range(4):
            out[z, 64 + i * 8 : 72 + i * 8, :] = small[i][z * 8 : (z + 1) * 8]


def lane_sums(value):
    rows = jnp.sum(value, axis=0, keepdims=True)
    return sum(rows[:, t * 128 : (t + 1) * 128] for t in range(value.shape[1] // 128))


def field_product(a, b):
    return lane_sums(a[0] * b[0] + a[1] * b[1])


def middle_kernel(
    got, field_in, d_in, w1_in, own, places_in, column, parent, out, r0_out, br_out
):
    total = sum(got[z, 0:48, :] for z in range(4))
    small = sum(got[z, 64:96, :] for z in range(4))
    v0, v1, v2 = (total[i * 16 : (i + 1) * 16] for i in range(3))

    def repeated(value):
        return jnp.concatenate(
            [jnp.broadcast_to(value[w : w + 1], (2, 256)) for w in range(8)], axis=0
        )

    y0, w2, w3, n = (own[i * 16 : (i + 1) * 16, :] for i in range(4))
    lane = iota((256, 256), 0)
    at = parent[...] // 4 * 32 + parent[...] % 4
    vd, vd2, e = (repeated(small[i * 8 : (i + 1) * 8]) for i in range(3))
    vw, vw2 = (repeated(dot(small[24:32], flag(lane == at + i))) for i in (8, 12))
    same = same_parent(parent[...], column[...])
    g0 = v0 + n * y0
    shared = dot(jnp.concatenate([y0, e * y0, g0], axis=0), same)
    b1 = v1 + vd * y0 + vw * shared[0:16]
    b2 = v2 + vd2 * y0 + (e + vw2) * shared[0:16] + shared[16:32]
    y1 = w2 * g0 + w3 * shared[32:48]
    g1 = b1 + n * y1
    shared = dot(jnp.concatenate([y1, g1], axis=0), same)
    k1 = vd * y1 + vw * shared[0:16]
    y2 = w2 * g1 + w3 * shared[16:32]
    m1 = lane_sums(g0 * y1)
    m2 = lane_sums((2.0 * b1 + n * y1) * y1)
    m3 = lane_sums((2.0 * b2 + k1) * y1 + g1 * y2)

    d, w1 = d_in[...], w1_in[...]
    shares = jnp.concatenate([got[z, 48:64, :] for z in range(4)], axis=0)
    lifted = lifted_categories(shares, places_in[...])
    field = steps(field_in)
    r0 = [field[h] + lifted[h] for h in range(2)]
    br = mixed(r0, d, w1, same)
    for h in range(2):
        r0_out[h * 256 : (h + 1) * 256, :] = r0[h]
        br_out[h * 256 : (h + 1) * 256, :] = br[h]
    m0 = field_product(r0, r0)
    m1 += field_product(r0, br)
    m2 += field_product(br, br)
    m3 += field_product(br, mixed(br, d, w1, same))
    moments = jnp.concatenate([m0, m1, m2, m3, jnp.zeros((4, 128), F32)], axis=0)
    moments = jnp.sum(moments, axis=1, keepdims=True)
    at_lane = iota((8, 128), 0) == iota((8, 128), 1)
    moments = jnp.sum(jnp.where(at_lane, moments, 0.0), axis=0, keepdims=True)
    for z in range(4):
        at = z * 66
        for t in range(2):
            out[at + t * 16 : at + (t + 1) * 16, :] = y1[:, t * 128 : (t + 1) * 128]
            out[at + 32 + t * 16 : at + 48 + t * 16, :] = y2[:, t * 128 : (t + 1) * 128]
        out[at + 64 : at + 66, :] = jnp.concatenate([moments] * 2, axis=0)


def fields_kernel(got, r0_in, br_in, d_in, w1_in, places_in, column, parent, out):
    same, category = same_parent(parent[...], column[...]), places_in[...]

    def shares(first):
        tiles = [
            jnp.concatenate([got[z * 66 + at : z * 66 + at + 16, :] for z in range(4)], axis=0)
            for at in (first, first + 16)
        ]
        return jnp.concatenate(tiles, axis=1)

    first = lifted_categories(shares(0), category)
    second = lifted_categories(shares(32), category)
    br = steps(br_in)
    field = [br[h] + first[h] for h in range(2)]
    after = mixed(field, d_in[...], w1_in[...], same)
    after = [after[h] + second[h] for h in range(2)]
    moments = sum(got[z * 66 + 64 : z * 66 + 65, :] for z in range(4))
    rows = []
    for one in (steps(r0_in), field, after):
        for half in range(2):
            lanes = slice(half * 128, (half + 1) * 128)
            tiles = [v.reshape(8, 4, 8, 256) for v in one]
            k = [jnp.concatenate([t[:, i] for t in tiles], axis=0) for i in range(4)]
            k = [v.reshape(128, 256)[:, lanes] for v in k]
            rows += [jnp.concatenate(k[0:2], axis=1), jnp.concatenate(k[2:4], axis=1)]
    rows = jnp.concatenate(rows, axis=0)
    source, target = iota((256, 256), 0), iota((256, 256), 1)
    group = source // 32
    place = (group & 1) * 128 + ((group & 2) | (group // 4)) * 32 + source % 32
    moves = flag(target == place)
    high = rows.astype(BF16)
    rest = rows - high.astype(F32)
    rows = jnp.dot(
        jnp.concatenate([high, *parts(rest)], axis=1),
        jnp.concatenate([moves] * 3, axis=0),
        preferred_element_type=F32,
    )
    upper = iota((128, 128), 1) >= 64
    for i in range(3):
        for half in range(2):
            at = (i * 2 + half) * 256
            pieces = [None] * 4
            for j in range(2):
                a, b = (rows[at + p : at + p + 128, j * 128 : (j + 1) * 128] for p in (0, 128))
                moved = pltpu.roll(jnp.where(upper, a, b), 64, 1)
                pieces[j] = jnp.where(upper, moved, a)
                pieces[j + 2] = jnp.where(upper, b, moved)
            for g in range(4):
                for w in range(8):
                    to = sender(half * 4 + g, w) * 49 + i * 16
                    for h in range(2):
                        out[to + h * 8 : to + h * 8 + 8, :] = pieces[g][
                            (h * 8 + w) * 8 : (h * 8 + w) * 8 + 8
                        ]
    for s in range(64):
        out[s * 49 + 48 : s * 49 + 49, :] = moments


def finish_kernel(got, x_out, r_out, x_ref, r_ref, turned, sems):
    sums = [
        sum(got[s * 49 + 48 : s * 49 + 49, :] for s in range(i, 64, 8)) for i in range(8)
    ]
    m = sum(sums)
    m0, m1, m2, m3 = (m[:, i : i + 1] for i in range(4))
    alpha = m0 / m1
    norm = m0 - 2.0 * alpha * m1 + alpha * alpha * m2
    grown = 1.0 + norm / m0
    product = grown * grown * m1 - 2.0 * grown * alpha * m2 + alpha * alpha * m3
    later = norm / product
    on_first, on_second = alpha + later * grown, -later * alpha
    for s in range(64):
        first, second, third = (got[s * 49 + i * 16 : s * 49 + i * 16 + 16, :] for i in range(3))
        x_ref[s * 16 : (s + 1) * 16, :] = on_first * first + on_second * second
        r_ref[s * 16 : (s + 1) * 16, :] = first - on_first * second - on_second * third
    copies = []
    for j, (ref, out) in enumerate(((x_ref, x_out), (r_ref, r_out))):
        for i in range(8):
            block = ref[pl.ds(i, 128, stride=8), :].T
            for k in range(4):
                turned[pl.ds(j * 1024 + k * 8 + i, 32, stride=32), :] = block[
                    k * 32 : (k + 1) * 32
                ]
        copy = pltpu.make_async_copy(turned.at[pl.ds(j * 1024, 1024), :], out, sems.at[j])
        copy.start()
        copies.append(copy)
    for copy in copies:
        copy.wait()


def call(kernel, outs, scratch=(), kept=(), last=False):
    vmem = pl.BlockSpec(memory_space=pltpu.VMEM)
    kind = jax.ShapeDtypeStruct if last else pltpu.VMEM

    def run(*args):
        args = [
            pltpu.with_memory_space_constraint(a, pltpu.VMEM) if i in kept else a
            for i, a in enumerate(args)
        ]
        return pl.pallas_call(
            kernel,
            out_shape=tuple(kind(shape, F32) for shape in outs),
            in_specs=[vmem] * len(args),
            out_specs=(pl.BlockSpec(memory_space=pl.ANY) if last else vmem,) * len(outs),
            scratch_shapes=[pltpu.VMEM(shape, F32) for shape in scratch]
            + [pltpu.SemaphoreType.DMA((2,))] * last,
            compiler_params=pltpu.CompilerParams(vmem_limit_bytes=(16 if kept else 58) << 20),
        )(*args)

    return run


def exchanged(value, axes, blocks, tile):
    shape = value.shape
    value = value.reshape(blocks, -1, tile, shape[-1])
    return lax.all_to_all(value, axes, 0, 0, tiled=True).reshape(shape)


def row_of(table, wanted, names):
    hit = table[:, :, None] == wanted[None, None, :]
    return jnp.sum(jnp.where(hit, names[:, None, None], 0), axis=(0, 1), dtype=jnp.int32)[None]


def on_device(b, gi, ac, gc, d, w1, w2, w3, group_table, class_table):
    (sent,) = call(pack_kernel, [(64 * 28, 128)], [(1024, 128), (128, 128)])(
        b.reshape(1024, 128),
        d,
        gi.reshape(128, 128),
        w1,
        ac.reshape(32, 128),
        w2.reshape(1, 32),
        gc,
        w3,
    )
    got = exchanged(sent, SPLIT, 64, 4)
    category = jnp.arange(32, dtype=jnp.int32)
    lane = jnp.arange(256, dtype=jnp.int32)
    parent = row_of(group_table, lane, category)
    product = lane // 64 * 256 + lax.axis_index("far") * 64 + lane % 64
    place = category % 8 // 2 * 8 + category // 8 * 2 + category % 2
    gam = row_of(class_table, product, place)
    sent, field, d_all, w1_all, own, places, column = call(
        spread_kernel,
        [(4, 96, 256), (512, 256), (256, 256), (256, 256), (64, 256), (256, 128), (256, 128)],
        [(128, 256), (128, 256)],
        kept=(0,),
    )(got, parent, gam, class_table)
    got = exchanged(sent, "far", 4, 8)
    sent, r0, br = call(middle_kernel, [(4 * 66, 128), (512, 256), (512, 256)], kept=range(7))(
        got, field, d_all, w1_all, own, places, column, parent
    )
    got = exchanged(sent, "far", 4, 2)
    (sent,) = call(fields_kernel, [(64 * 49, 128)], kept=range(7))(
        got, r0, br, d_all, w1_all, places, column, parent
    )
    got = exchanged(sent, SPLIT, 64, 1)
    solution_field, residual = call(
        finish_kernel,
        [(1024, 128)] * 2,
        [(1024, 128), (1024, 128), (2048, 128)],
        kept=(0,),
        last=True,
    )(got)
    return solution_field.reshape(32, 32, 128), residual.reshape(32, 32, 128)


def solution(mesh):
    finer = Mesh(
        mesh.devices.reshape(4, 2, 4, 4, 2), ("y", "core", "x", "far", "near")
    )
    return jax.shard_map(
        on_device,
        mesh=finer,
        in_specs=(
            P(REG, PROD, None),
            P(REG, PROD, None),
            P(REG, PROD, None),
            P(REG, None, None),
            P(REG, PROD),
            P(REG, PROD),
            P(REG, PROD),
            P(REG, None),
            P(),
            P(),
        ),
        out_specs=(P(REG, PROD, None), P(REG, PROD, None)),
        check_vma=False,
    )
```
